32 devices in a mesh: row: 8 (over z, core), col: 4 (over y, x).
Axes of the slice: x: 2, y: 2, z: 4, core: 2. Of those that a mesh axis runs over, the one named last changes fastest.
Arguments:
- points: bfloat16 [2048, 1024], P(('row', 'col')), may hold values from -6 to 6
- factor: float32 [2048, 256], P(('row', 'col')), may hold values from 0 to 1
Outputs:
- factor_out: float32 [2048, 256], P(('row', 'col'))
The draws below stay inside these ranges and needn't reach their ends.
All inputs are finite; a program needn't handle non-finite values.
Results may differ from the reference program's by a relative error of at most 0.002.
The reference program's roundings to bfloat16 on the way count: a program that leaves them out, or rounds other values in their place, can miss the bound.
Values may be sent and summed in bfloat16 or wider, within the bound.
A program may use at most 64 MiB of HBM per device.

```python
import math
import jax
import jax.numpy as jnp
from jax import lax

EMBED_WIDTH = 1024
R = 256
ITERS = 2
NPTS = 2048


def level_of(key, shape, split, least, top_value):
    factor_of, own = 1.0, jax.random.fold_in(key, 6)
    for axis_at, blocks in split:
        steps = jnp.exp(jax.random.uniform(jax.random.fold_in(own, axis_at), (blocks,), jnp.float32, least / len(split), top_value / len(split)))
        factor_of = factor_of * jnp.repeat(steps, shape[axis_at] // blocks).reshape([-1 if axis == axis_at else 1 for axis in range(len(shape))])
    return factor_of


def gaussian(rng, dims, spread, reach, shards=(), kind=jnp.bfloat16):
    entries = jax.random.normal(rng, dims, jnp.float32) * spread
    if len(shards) > 0:
        entries = level_of(rng, dims, shards, -0.22, 0.18) * entries
    return jnp.clip(entries, min=-reach, max=reach).astype(kind)


def setup_inputs(seed: int = 0) -> dict:
    arg_keys = jax.random.split(jax.random.key(seed), 3)
    points = gaussian(arg_keys[0], (NPTS, EMBED_WIDTH), 1.0, 6.0, ((0, 32),))
    factor = jnp.clip(1.0 * jax.random.uniform(arg_keys[1], (NPTS, R), jnp.float32) ** level_of(arg_keys[1], (NPTS, R), ((0, 32),), -0.2, 0.2), 0.0, 1.0)
    return dict(points=points, factor=factor)


def reference(points, factor):
    data = points.astype(jnp.float32)
    total = data.shape[0]
    rank = factor.shape[1]
    block_slab = math.gcd(512, total)
    nblocks = total // block_slab
    squared_norms = lax.optimization_barrier(jnp.sum(data * data, axis=1))

    def kernel_row_slab(index):
        offset_begin = (index * block_slab).astype(jnp.int32)
        rows = lax.dynamic_slice_in_dim(data, offset_begin, block_slab, 0)
        row_squared_norm = lax.dynamic_slice_in_dim(squared_norms, offset_begin, block_slab, 0)
        gram_matrix = jnp.dot(rows, data.T, precision=lax.Precision.HIGHEST)
        return jnp.exp((2.0 * gram_matrix - row_squared_norm[:, None] - squared_norms[None, :]) * (0.5 / EMBED_WIDTH))
    indices = jnp.arange(nblocks, dtype=jnp.int32)
    rowsum = lax.map(lambda i: lax.optimization_barrier(jnp.sum(kernel_row_slab(i), axis=1)), indices).reshape(total)
    grand = jnp.sum(rowsum)
    means = rowsum / total

    def affinity_rows(index):
        offset_begin = (index * block_slab).astype(jnp.int32)
        kern = kernel_row_slab(index)
        mine = lax.dynamic_slice_in_dim(means, offset_begin, block_slab, 0)
        return (kern - mine[:, None] - means[None, :] + grand / (total * total)).astype(jnp.bfloat16)
    unit = 2.0 / math.sqrt(total * rank)
    h = factor * unit
    for step in range(ITERS):
        hb = lax.optimization_barrier(h.astype(jnp.bfloat16)).astype(jnp.float32)
        ah = lax.map(lambda i: jnp.dot(affinity_rows(i).astype(jnp.float32), hb, precision=lax.Precision.HIGHEST), indices).reshape(total, rank)
        hh = jnp.dot(h.T, h, precision=lax.Precision.HIGHEST)
        scale = 0.5 / jnp.sqrt(jnp.sum(hh * hh) + 1e-06)
        h = jnp.maximum(h - scale * (jnp.dot(h, hh, precision=lax.Precision.HIGHEST) - ah), 0.0)
    return h / unit
```

```python
import functools
import math

import jax
import jax.numpy as jnp
from jax import lax
from jax.experimental import pallas as pl
from jax.experimental.pallas import tpu as pltpu
from jax.sharding import PartitionSpec as P

MESH = pl.DeviceIdType.MESH

SENDS = ("rpts", "cpts", "first", "later", "rsum", "csum", "tsum", "aff")


def layout(nrow, ncol):
    side, nz = math.isqrt(ncol), nrow // 2
    low = 2 if nz % 2 == 0 else 1
    return side, low, nz // low


def cuts_of(rows):
    return 4 if rows % 64 == 0 else 1


def receive_keys(nrow, ncol, rows):
    side, low, high = layout(nrow, ncol)
    cuts = cuts_of(rows)
    relayed = (cuts + 1) // 2
    keys = [("rx", k) for k in range(1, side)]
    keys += [("rl", k, c) for k in range(1, low) for c in range(cuts)]
    keys += [("rd", l, k, c) for l in range(1, low) for k in range(1, side) for c in range(min(relayed + 1, cuts))]
    keys += [("cy", k) for k in range(1, side)]
    keys += [("ch", k, c) for k in range(1, high) for c in range(cuts)]
    keys += [("cd", h, k, c) for h in range(1, high) for k in range(1, side) for c in range(cuts)]
    keys += [("cp", h, k) for h in range(high) for k in range(side)]
    keys += [("rsum",), ("csum",), ("tsum",)]
    keys += [("aff", k) for k in range(1, side * low)]
    for name in ("first", "later"):
        keys += [(name, "z", k) for k in range(1, low * high)]
        keys += [(name, "plane", k, p) for k in range(low * high) for p in range(1, side * side)]
        keys += [(name, "partner", k) for k in range(low * high)]
    return {key: i for i, key in enumerate(keys)}


def shift(i, k, n, sign):
    if n & (n - 1) or n == 2:
        return (i + sign * k + n) % n
    out, bit = i, 1
    while bit < n:
        if k & bit:
            out = out + bit - 2 * bit * ((i // bit) % 2)
        bit *= 2
    return out


def kernel(nrow, ncol, keys, pts_ref, fac_ref, out_ref, rbuf, cbuf, first, later, kern, asend, arecv, rsum, csum, tsum, ssem, rsem):
    side, low, high = layout(nrow, ncol)
    nz = low * high
    rows, width = pts_ref.shape
    rank = fac_ref.shape[1]
    wide = 2 * rows
    nr, nc = low * side, high * side
    total = rows * nrow * ncol
    unit = 2.0 / math.sqrt(total * rank)
    cuts = cuts_of(rows)
    relayed = (cuts + 1) // 2
    piece = rows // cuts
    row, col = lax.axis_index("row"), lax.axis_index("col")
    z, core = row // 2, row % 2
    zh, zl = z // low, z % low
    y, x = col // side, col % side
    rid, cid = zl * side + x, zh * side + y
    partner = (z * 2 + 1 - core, col)

    def slot(r, c):
        return (r * nc + c) * 2 + core

    def device(h, l, yy, xx):
        return ((h * low + l) * 2 + core, yy * side + xx)

    def at_h(k, sign):
        return shift(zh, k, high, sign)

    def at_l(k, sign):
        return shift(zl, k, low, sign)

    def at_y(k, sign):
        return (y + sign * k + side) % side

    def at_x(k, sign):
        return (x + sign * k + side) % side

    def remote(src, dst, kind, key, where):
        return pltpu.make_async_remote_copy(
            src_ref=src,
            dst_ref=dst,
            send_sem=ssem.at[SENDS.index(kind)],
            recv_sem=rsem.at[keys[key]],
            device_id=where,
            device_id_type=MESH,
        )

    def send(src, dst, kind, key, where):
        remote(src, dst, kind, key, where).start()

    def arrive(block, kind, key):
        remote(block, block, kind, key, partner).wait_recv()

    barrier = pltpu.get_barrier_semaphore()
    peers = [device(zh, zl, y, at_x(k, 1)) for k in range(1, side)]
    peers += [device(zh, zl, at_y(k, 1), x) for k in range(1, side)]
    peers += [device(zh, at_l(k, 1), y, x) for k in range(1, low)]
    peers += [device(at_h(k, 1), zl, y, x) for k in range(1, high)]
    peers += [device(zh, at_l(l, 1), y, at_x(k, 1)) for l in range(1, low) for k in range(1, side)]
    peers.append(partner)
    for peer in peers:
        pl.semaphore_signal(barrier, inc=1, device_id=peer, device_id_type=MESH)
    h = fac_ref[...] * unit
    first[slot(rid, cid)] = h.astype(jnp.bfloat16)
    rbuf[rid] = pts_ref[...]
    cbuf[cid * 2 + core] = pts_ref[...]
    pl.semaphore_wait(barrier, len(peers))

    def part(c, n=1):
        return pl.ds(c * piece, n * piece)

    for c in range(cuts):
        for k in range(1, high):
            send(pts_ref.at[part(c)], cbuf.at[cid * 2 + core, part(c)], "cpts", ("ch", k, c), device(at_h(k, 1), zl, y, x))
    for k in range(1, side):
        send(pts_ref, rbuf.at[rid], "rpts", ("rx", k), device(zh, zl, y, at_x(k, 1)))
        send(pts_ref, cbuf.at[cid * 2 + core], "cpts", ("cy", k), device(zh, zl, at_y(k, 1), x))
    send(pts_ref, cbuf.at[cid * 2 + core], "cpts", ("cp", 0, 0), partner)
    for c in range(cuts):
        for k in range(1, low):
            send(pts_ref.at[part(c)], rbuf.at[rid, part(c)], "rpts", ("rl", k, c), device(zh, at_l(k, 1), y, x))
    if relayed < cuts:
        rest = part(relayed, cuts - relayed)
        for l in range(1, low):
            for k in range(1, side):
                there = device(zh, at_l(l, 1), y, at_x(k, 1))
                send(pts_ref.at[rest], rbuf.at[rid, rest], "rpts", ("rd", l, k, relayed), there)

    def column_peer(k):
        block = cbuf.at[(zh * side + at_y(k, -1)) * 2 + core]
        arrive(block, "cpts", ("cy", k))
        send(block, block, "cpts", ("cp", 0, k), partner)

    for c in range(cuts):
        if c == cuts - 1:
            for k in range(1, side):
                column_peer(k)
        for k in range(1, high):
            block = cbuf.at[(at_h(k, -1) * side + y) * 2 + core, part(c)]
            arrive(block, "cpts", ("ch", k, c))
            for ky in range(1, side):
                send(block, block, "cpts", ("cd", k, ky, c), device(zh, zl, at_y(ky, 1), x))
    for k in range(1, high):
        block = cbuf.at[(at_h(k, -1) * side + y) * 2 + core]
        send(block, block, "cpts", ("cp", k, 0), partner)
    for c in range(cuts):
        for k in range(1, low):
            block = rbuf.at[at_l(k, -1) * side + x, part(c)]
            if c < relayed:
                arrive(block, "rpts", ("rl", k, c))
                for kx in range(1, side):
                    send(block, block, "rpts", ("rd", k, kx, c), device(zh, zl, y, at_x(kx, 1)))
    for k in range(1, side):
        arrive(rbuf.at[zl * side + at_x(k, -1)], "rpts", ("rx", k))

    offsets = [(h, l) for h in range(high) for l in range(low)]
    plane = [(ky, kx) for ky in range(side) for kx in range(side)]

    class Gather:
        def __init__(self, ref, name):
            self.ref, self.name = ref, name

        def block(self, n, p):
            (kh, kl), (ky, kx) = offsets[n], plane[p]
            r, c = at_l(kl, -1) * side + at_x(kx, -1), at_h(kh, -1) * side + at_y(ky, -1)
            return self.ref.at[slot(r, c)]

        def along_z(self):
            for n in range(nz - 1, 0, -1):
                kh, kl = offsets[n]
                block = self.block(0, 0)
                send(block, block, self.name, (self.name, "z", n), device(at_h(kh, 1), at_l(kl, 1), y, x))

        def over_plane(self, n):
            block = self.block(n, 0)
            if n:
                arrive(block, self.name, (self.name, "z", n))
            for p in range(side * side - 1, 0, -1):
                ky, kx = plane[p]
                send(block, block, self.name, (self.name, "plane", n, p), device(zh, zl, at_y(ky, 1), at_x(kx, 1)))
            send(block, block, self.name, (self.name, "partner", n), partner)

        def to_partner(self, n):
            for p in range(1, side * side):
                block = self.block(n, p)
                arrive(block, self.name, (self.name, "plane", n, p))
                send(block, block, self.name, (self.name, "partner", n), partner)

        def finish(self, n):
            arrive(self.ref.at[pl.ds(0, side * side)], self.name, (self.name, "partner", n))
            kh, kl = offsets[n]
            return at_h(kh, -1), at_l(kl, -1)

    gather = Gather(first, "first")
    gather.along_z()
    gather.over_plane(0)

    def squares(block):
        acc = None
        for k in range(0, width, 128):
            one = block[:, k : k + 128].astype(jnp.float32)
            acc = one * one if acc is None else acc + one * one
        return acc

    row_sq, col_sq, row_acc, col_acc = {}, {}, {}, {}

    def tile(kl, kh):
        l, hh = at_l(kl, -1), at_h(kh, -1)
        mat = rbuf[pl.ds(l * side, side)].reshape(side * rows, width)
        block = cbuf[pl.ds(hh * side * 2, side * 2)].reshape(side * wide, width)
        if kl not in row_sq:
            row_sq[kl] = jnp.sum(squares(mat), axis=1, keepdims=True)
        if kh not in col_sq:
            col_sq[kh] = jnp.sum(squares(block).T, axis=0, keepdims=True)
        gram = lax.dot_general(mat, block, (((1,), (1,)), ((), ())), preferred_element_type=jnp.float32)
        k = jnp.exp((2.0 * gram - row_sq[kl] - col_sq[kh]) * (0.5 / width))
        kern[l, hh] = k
        folded = k[:, :128]
        for j in range(128, side * wide, 128):
            folded += k[:, j : j + 128]
        row_acc[kl] = row_acc[kl] + folded if kl in row_acc else folded
        below = jnp.sum(k, axis=0, keepdims=True)
        col_acc[kh] = col_acc[kh] + below if kh in col_acc else below

    def theirs(kh, ky):
        arrive(cbuf.at[(at_h(kh, -1) * side + at_y(ky, -1)) * 2 + 1 - core], "cpts", ("cp", kh, ky))

    for ky in range(side):
        theirs(0, ky)
    tile(0, 0)
    for kh in range(1, high):
        for ky in range(1, side):
            block = cbuf.at[(at_h(kh, -1) * side + at_y(ky, -1)) * 2 + core]
            for c in range(cuts):
                arrive(block.at[part(c)], "cpts", ("cd", kh, ky, c))
            send(block, block, "cpts", ("cp", kh, ky), partner)
    for kl in range(1, low):
        for c in range(relayed, cuts):
            arrive(rbuf.at[at_l(kl, -1) * side + x, part(c)], "rpts", ("rl", kl, c))
        for kx in range(1, side):
            block = rbuf.at[at_l(kl, -1) * side + at_x(kx, -1)]
            for c in range(relayed):
                arrive(block.at[part(c)], "rpts", ("rd", kl, kx, c))
            if relayed < cuts:
                arrive(block.at[part(relayed, cuts - relayed)], "rpts", ("rd", kl, kx, relayed))
        tile(kl, 0)
    for kh in range(1, high):
        for ky in range(side):
            theirs(kh, ky)
        for kl in range(low):
            tile(kl, kh)

    me_c = cid * 2 + core
    mydev = row * ncol + col
    tot = None
    for kh in range(high):
        csum[me_c, at_h(kh, -1)] = col_acc[kh]
        tot = col_acc[kh] if tot is None else tot + col_acc[kh]
    narrow = tot[:, :128]
    for j in range(128, side * wide, 128):
        narrow += tot[:, j : j + 128]
    tsum[mydev] = narrow
    for kl in range(low):
        rsum[rid, at_l(kl, -1)] = jnp.sum(row_acc[kl].T, axis=0, keepdims=True)

    def each(count, action):
        def body(k, carry):
            action(k)
            return carry

        lax.fori_loop(1, count, body, 0, unroll=count <= 32)

    def total_to(k):
        there = ((row + k // ncol) % nrow, (col + k % ncol) % ncol)
        send(tsum.at[mydev], tsum.at[mydev], "tsum", ("tsum",), there)

    each(nrow * ncol, total_to)
    for l in range(low):
        for k in range(side):
            if l or k:
                send(rsum.at[rid], rsum.at[rid], "rsum", ("rsum",), device(zh, at_l(l, 1), y, at_x(k, 1)))
    for kh in range(high):
        for ky in range(side):
            for flip in range(2):
                if kh or ky or flip:
                    there, cc = device(at_h(kh, 1), zl, at_y(ky, 1), x)
                    there = there + flip * (1 - 2 * core)
                    send(csum.at[me_c], csum.at[me_c], "csum", ("csum",), (there, cc))

    for n in range(1, nz):
        gather.over_plane(n)

    def gram_of(block):
        return lax.dot_general(block, block, (((0,), (0,)), ((), ())), preferred_element_type=jnp.float32)

    def pull(h, hh):
        scale = 0.5 / jnp.sqrt(jnp.sum(hh * hh, keepdims=True) + 1e-06)
        return scale, jnp.dot(h, hh, precision=lax.Precision.HIGHEST, preferred_element_type=jnp.float32)

    arrive(rsum.at[pl.ds(0, nr - 1)], "rsum", ("rsum",))
    arrive(csum.at[pl.ds(0, 2 * nc - 1)], "csum", ("csum",))
    arrive(tsum.at[pl.ds(0, nrow * ncol - 1)], "tsum", ("tsum",))
    grand = jnp.sum(jnp.sum(tsum[...], axis=0), axis=1, keepdims=True) / (total * total)
    col_mean = [jnp.sum(csum[:, i], axis=0) / total for i in range(high)]
    row_mean = [jnp.sum(rsum[:, i], axis=0) / total for i in range(low)]
    for l in range(low):
        mean_r = jnp.broadcast_to(row_mean[l], (128, side * rows)).T
        mean_r = jnp.concatenate([mean_r] * (side * wide // 128), axis=1)
        for i in range(high):
            a = (kern[l, i] - mean_r - col_mean[i] + grand).astype(jnp.bfloat16).reshape(side, rows, side * wide)
            for k in range(side):
                asend[l * side + k, i] = a[k]

    def affinity(l, k, sign):
        return at_l(l, sign) * side + at_x(k, sign)

    around = [(l, k) for l in range(low) for k in range(side)]
    for n in range(len(around) - 1, 0, -1):
        l, k = around[n]
        there = device(zh, at_l(l, 1), y, at_x(k, 1))
        send(asend.at[affinity(l, k, 1)], arecv.at[rid], "aff", ("aff", n), there)
    arecv[rid] = asend[rid]

    def panel(ref, r, i):
        return ref[pl.ds((r * nc + i * side) * 2, 2 * side)].reshape(side * wide, rank)

    for n in range(nz):
        gather.to_partner(n)
    hh = jnp.zeros((rank, rank), jnp.float32)
    for n in range(nz):
        i, l = gather.finish(n)
        for k in range(side):
            hh += gram_of(panel(first, l * side + k, i))
    scale, hhh = pull(h, hh)
    ah = jnp.zeros((rows, rank), jnp.float32)
    for n, (l, k) in enumerate(around):
        r = affinity(l, k, -1)
        if n:
            arrive(arecv.at[r], "aff", ("aff", n))
        for i in range(high):
            ah += jnp.dot(arecv[r, i], panel(first, r, i), preferred_element_type=jnp.float32)
    h = jnp.maximum(h - scale * (hhh - ah), 0.0)

    later[slot(rid, cid)] = h.astype(jnp.bfloat16)
    again = Gather(later, "later")
    again.along_z()
    again.over_plane(0)
    ah = jnp.zeros((rows, rank), jnp.float32)
    hh = jnp.zeros((rank, rank), jnp.float32)
    for n in range(1, nz):
        again.over_plane(n)
        again.to_partner(n - 1)
    again.to_partner(nz - 1)
    for n in range(nz):
        i, l = again.finish(n)
        for k in range(side):
            block = panel(later, l * side + k, i)
            ah += jnp.dot(arecv[l * side + k, i], block, preferred_element_type=jnp.float32)
            hh += gram_of(block)
    scale, hhh = pull(h, hh)
    out_ref[...] = jnp.maximum(h - scale * (hhh - ah), 0.0) / unit

    def sent(ref, kind, key):
        remote(ref, ref, kind, key, partner).wait_send()

    sent(rbuf.at[pl.ds(0, nr - 1)], "rpts", ("aff", 1))
    sent(cbuf.at[pl.ds(0, 2 * nc - 1)], "cpts", ("aff", 1))
    sent(first.at[pl.ds(0, nrow * ncol - 1)], "first", ("aff", 1))
    sent(later.at[pl.ds(0, nrow * ncol - 1)], "later", ("aff", 1))
    sent(rsum.at[pl.ds(0, nr - 1)], "rsum", ("aff", 1))
    sent(csum.at[pl.ds(0, 2 * nc - 1)], "csum", ("aff", 1))
    sent(tsum.at[pl.ds(0, nrow * ncol - 1)], "tsum", ("aff", 1))
    sent(asend.at[pl.ds(0, nr - 1)], "aff", ("aff", 1))


def solution(mesh):
    nrow, ncol = mesh.shape["row"], mesh.shape["col"]
    side, low, high = layout(nrow, ncol)

    def shards(points, factor):
        rows, width = points.shape
        rank = factor.shape[1]
        wide = 2 * rows
        nr, nc = low * side, high * side
        keys = receive_keys(nrow, ncol, rows)
        buffers = [
            ((nr, rows, width), jnp.bfloat16),
            ((2 * nc, rows, width), jnp.bfloat16),
            ((nrow * ncol, rows, rank), jnp.bfloat16),
            ((nrow * ncol, rows, rank), jnp.bfloat16),
            ((low, high, side * rows, side * wide), jnp.float32),
            ((nr, high, rows, side * wide), jnp.bfloat16),
            ((nr, high, rows, side * wide), jnp.bfloat16),
            ((nr, low, 1, side * rows), jnp.float32),
            ((2 * nc, high, 1, side * wide), jnp.float32),
            ((nrow * ncol, 1, 128), jnp.float32),
        ]
        held = sum(math.prod(shape) * jnp.dtype(kind).itemsize for shape, kind in buffers)
        return pl.pallas_call(
            functools.partial(kernel, nrow, ncol, keys),
            out_shape=jax.ShapeDtypeStruct((rows, rank), jnp.float32),
            in_specs=[pl.BlockSpec(memory_space=pltpu.VMEM)] * 2,
            out_specs=pl.BlockSpec(memory_space=pltpu.VMEM),
            scratch_shapes=[pltpu.VMEM(shape, kind) for shape, kind in buffers]
            + [pltpu.SemaphoreType.DMA((len(SENDS),)), pltpu.SemaphoreType.DMA((len(keys),))],
            compiler_params=pltpu.CompilerParams(
                collective_id=0, has_side_effects=True, vmem_limit_bytes=min(67043328, held + (16 << 20))
            ),
        )(points, factor)

    spec = P(("row", "col"), None)
    return jax.shard_map(shards, mesh=mesh, in_specs=(spec, spec), out_specs=spec, check_vma=False)
```

```python
import functools
import math

import jax
import jax.numpy as jnp
from jax import lax
from jax.experimental import pallas as pl
from jax.experimental.pallas import tpu as pltpu
from jax.sharding import PartitionSpec as P

MESH = pl.DeviceIdType.MESH

SENDS = ("rpts", "cpts", "rfac", "cfac", "later", "rsum", "csum", "tsum", "pull", "aff")


def layout(nrow, ncol):
    side, nz = math.isqrt(ncol), nrow // 2
    low = 2 if nz % 2 == 0 else 1
    return side, low, nz // low


def cuts_of(rows):
    return 4 if rows % 64 == 0 else 1


def receive_keys(nrow, ncol, rows):
    side, low, high = layout(nrow, ncol)
    cuts = cuts_of(rows)
    plane, nz = side * side, low * high
    keys = [(name, k) for name in ("rx",) for k in range(1, side)]
    keys += [("ry", k, c) for k in range(1, side) for c in range(cuts)]
    keys += [("rd", j, k, c) for j in range(1, side) for k in range(1, side) for c in range(cuts)]
    keys += [(name, k) for name in ("cl", "hl") for k in range(1, low)]
    keys += [("ch", k, c) for k in range(1, high) for c in range(cuts)]
    keys += [("hz", k) for k in range(1, high)]
    keys += [(name, h, k, c) for name in ("cd", "ce") for h in range(1, high) for k in range(1, low) for c in range(cuts)]
    keys += [(name, h, k) for name in ("hd", "he") for h in range(1, high) for k in range(1, low)]
    keys += [(name, h, k) for name in ("cp", "hp") for h in range(high) for k in range(low) if not h or not k]
    keys += [("rsum",), ("csum",), ("tsum",)]
    keys += [(name, k) for name in ("aff", "pull", "hr") for k in range(1, plane)]
    keys += [("z", k) for k in range(1, nz)]
    keys += [("plane", k, p) for k in range(nz) for p in range(1, plane)]
    keys += [("partner", k) for k in range(nz)]
    return {key: i for i, key in enumerate(keys)}


def snake(h, l, low):
    return l + (h % 2) * (low - 1 - 2 * l)


def shift(i, k, n, sign):
    if n & (n - 1) or n == 2:
        return (i + sign * k + n) % n
    out, bit = i, 1
    while bit < n:
        if k & bit:
            out = out + bit - 2 * bit * ((i // bit) % 2)
        bit *= 2
    return out


def kernel(nrow, ncol, keys, pts_ref, fac_ref, out_ref, rbuf, cbuf, hr, hc, later, kern, psend, precv, asend, arecv, means, rsum, csum, tsum, ssem, rsem):
    side, low, high = layout(nrow, ncol)
    nz = low * high
    rows, width = pts_ref.shape
    rank = fac_ref.shape[1]
    wide = 2 * rows
    nr, nc = side * side, nz
    total = rows * nrow * ncol
    unit = 2.0 / math.sqrt(total * rank)
    cuts = cuts_of(rows)
    piece = rows // cuts
    row, col = lax.axis_index("row"), lax.axis_index("col")
    z, core = row // 2, row % 2
    zh = z // low
    zl = snake(zh, z % low, low)
    y, x = col // side, col % side
    rid, cid = y * side + x, zh * low + zl
    partner = (z * 2 + 1 - core, col)

    def device(h, l, yy, xx):
        return ((h * low + snake(h, l, low)) * 2 + core, yy * side + xx)

    def at_h(k, sign):
        return shift(zh, k, high, sign)

    def at_l(k, sign):
        return shift(zl, k, low, sign)

    def at_y(k, sign):
        return (y + sign * k + side) % side

    def at_x(k, sign):
        return (x + sign * k + side) % side

    def column(kh, kl):
        return at_h(kh, -1) * low + at_l(kl, -1)

    def remote(src, dst, kind, key, where):
        return pltpu.make_async_remote_copy(
            src_ref=src,
            dst_ref=dst,
            send_sem=ssem.at[SENDS.index(kind)],
            recv_sem=rsem.at[keys[key]],
            device_id=where,
            device_id_type=MESH,
        )

    def send(src, dst, kind, key, where):
        remote(src, dst, kind, key, where).start()

    def arrive(block, kind, key):
        remote(block, block, kind, key, partner).wait_recv()

    plane = [(ky, kx) for ky in range(side) for kx in range(side)]

    def row_peer(n, sign):
        ky, kx = plane[n]
        return at_y(ky, sign) * side + at_x(kx, sign)

    def in_plane(n):
        ky, kx = plane[n]
        return device(zh, zl, at_y(ky, 1), at_x(kx, 1))

    barrier = pltpu.get_barrier_semaphore()
    peers = [in_plane(n) for n in range(1, nr)]
    peers += [device(zh, at_l(k, 1), y, x) for k in range(1, low)]
    peers += [device(at_h(k, 1), zl, y, x) for k in range(1, high)]
    peers.append(partner)
    for peer in peers:
        pl.semaphore_signal(barrier, inc=1, device_id=peer, device_id_type=MESH)
    h = fac_ref[...] * unit
    hb = h.astype(jnp.bfloat16)
    hr[rid] = hb
    hc[cid * 2 + core] = hb
    rbuf[rid] = pts_ref[...]
    cbuf[cid * 2 + core] = pts_ref[...]
    pl.semaphore_wait(barrier, len(peers))

    def part(c):
        return pl.ds(c * piece, piece)

    mine, own = hc.at[cid * 2 + core], cbuf.at[cid * 2 + core]
    for k in range(1, high):
        send(mine, mine, "cfac", ("hz", k), device(at_h(k, 1), zl, y, x))
    for c in range(cuts):
        for k in range(1, high):
            send(pts_ref.at[part(c)], own.at[part(c)], "cpts", ("ch", k, c), device(at_h(k, 1), zl, y, x))
    for c in range(cuts):
        for k in range(1, side):
            send(pts_ref.at[part(c)], rbuf.at[rid, part(c)], "rpts", ("ry", k, c), device(zh, zl, at_y(k, 1), x))
    for k in range(1, side):
        send(pts_ref, rbuf.at[rid], "rpts", ("rx", k), device(zh, zl, y, at_x(k, 1)))
    for k in range(1, low):
        send(pts_ref, own, "cpts", ("cl", k), device(zh, at_l(k, 1), y, x))
        send(mine, mine, "cfac", ("hl", k), device(zh, at_l(k, 1), y, x))
    send(pts_ref, own, "cpts", ("cp", 0, 0), partner)
    send(mine, mine, "cfac", ("hp", 0, 0), partner)
    for n in range(1, nr):
        send(hr.at[rid], hr.at[rid], "rfac", ("hr", n), in_plane(n))

    for k in range(1, high):
        block = hc.at[column(k, 0) * 2 + core]
        arrive(block, "cfac", ("hz", k))
        for kl in range(1, low):
            send(block, block, "cfac", ("hd", k, kl), device(zh, at_l(kl, 1), y, x))
        send(block, block, "cfac", ("hp", k, 0), partner)
    for c in range(cuts):
        for k in range(1, side):
            block = rbuf.at[at_y(k, -1) * side + x, part(c)]
            arrive(block, "rpts", ("ry", k, c))
            for kx in range(1, side):
                send(block, block, "rpts", ("rd", k, kx, c), device(zh, zl, y, at_x(kx, 1)))
        if c == cuts - 1:
            for k in range(1, low):
                block = hc.at[column(0, k) * 2 + core]
                arrive(cbuf.at[column(0, k) * 2 + core], "cpts", ("cl", k))
                send(cbuf.at[column(0, k) * 2 + core], cbuf.at[column(0, k) * 2 + core], "cpts", ("cp", 0, k), partner)
                arrive(block, "cfac", ("hl", k))
                send(block, block, "cfac", ("hp", 0, k), partner)
        for k in range(1, high):
            block = cbuf.at[column(k, 0) * 2 + core, part(c)]
            arrive(block, "cpts", ("ch", k, c))
            for kl in range(1, low):
                send(block, block, "cpts", ("cd", k, kl, c), device(zh, at_l(kl, 1), y, x))
    for k in range(1, high):
        block = cbuf.at[column(k, 0) * 2 + core]
        send(block, block, "cpts", ("cp", k, 0), partner)

    def squares(block):
        acc = None
        for k in range(0, width, 128):
            one = block[:, k : k + 128].astype(jnp.float32)
            acc = one * one if acc is None else acc + one * one
        return acc

    row_sq, col_sq, row_acc, col_acc, forces = {}, {}, {}, {}, {}
    moment = jnp.zeros((1, rank), jnp.float32)
    spread = jnp.zeros((1, 128), jnp.float32)
    weight = jnp.zeros((1, rank), jnp.float32)

    def fold(a):
        out = a[:, :128]
        for j in range(128, a.shape[1], 128):
            out += a[:, j : j + 128]
        return out

    def split(a):
        near = a.astype(jnp.bfloat16)
        return near, (a - near.astype(jnp.float32)).astype(jnp.bfloat16)

    def tile(ky, kh):
        nonlocal moment, spread, weight
        yy, hh = at_y(ky, -1), at_h(kh, -1)
        mat = rbuf[pl.ds(yy * side, side)].reshape(side * rows, width)
        block = cbuf[pl.ds(hh * low * 2, low * 2)].reshape(low * wide, width)
        hrow = hr[pl.ds(yy * side, side)].reshape(side * rows, rank)
        hcol = hc[pl.ds(hh * low * 2, low * 2)].reshape(low * wide, rank)
        if ky not in row_sq:
            row_sq[ky] = jnp.sum(squares(mat), axis=1, keepdims=True)
        if kh not in col_sq:
            col_sq[kh] = jnp.sum(squares(block).T, axis=0, keepdims=True)
            weight += jnp.sum(hcol.astype(jnp.float32), axis=0, keepdims=True)
        inner = lax.dot_general(hrow, hcol, (((1,), (1,)), ((), ())), preferred_element_type=jnp.float32)
        spread += jnp.sum(fold(inner * inner), axis=0, keepdims=True)
        gram = lax.dot_general(mat, block, (((1,), (1,)), ((), ())), preferred_element_type=jnp.float32)
        k = jnp.exp((2.0 * gram - row_sq[ky] - col_sq[kh]) * (0.5 / width))
        kern[yy, hh] = k
        left = jnp.concatenate([*split(k), *split(inner)], axis=0)
        prod = jnp.dot(left, hcol, preferred_element_type=jnp.float32)
        n = side * rows
        drawn = prod[:n] + prod[n : 2 * n]
        moment += jnp.sum(drawn, axis=0, keepdims=True)
        force = prod[2 * n : 3 * n] + prod[3 * n :] - drawn
        forces[ky] = forces[ky] + force if ky in forces else force
        folded = fold(k)
        row_acc[ky] = row_acc[ky] + folded if ky in row_acc else folded
        below = jnp.sum(k, axis=0, keepdims=True)
        col_acc[kh] = col_acc[kh] + below if kh in col_acc else below

    for k in range(1, side):
        arrive(rbuf.at[y * side + at_x(k, -1)], "rpts", ("rx", k))
    for n in range(1, nr):
        arrive(hr.at[row_peer(n, -1)], "rfac", ("hr", n))
    for kl in range(low):
        arrive(cbuf.at[column(0, kl) * 2 + 1 - core], "cpts", ("cp", 0, kl))
        arrive(hc.at[column(0, kl) * 2 + 1 - core], "cfac", ("hp", 0, kl))
    tile(0, 0)
    for ky in range(1, side):
        for kx in range(1, side):
            for c in range(cuts):
                arrive(rbuf.at[at_y(ky, -1) * side + at_x(kx, -1), part(c)], "rpts", ("rd", ky, kx, c))
        tile(ky, 0)
    for kh in range(1, high):
        for kl in range(1, low):
            block = hc.at[column(kh, kl) * 2 + core]
            arrive(block, "cfac", ("hd", kh, kl))
            send(block, block, "cfac", ("he", kh, kl), partner)
            for c in range(cuts):
                block = cbuf.at[column(kh, kl) * 2 + core, part(c)]
                arrive(block, "cpts", ("cd", kh, kl, c))
                send(block, block, "cpts", ("ce", kh, kl, c), partner)
        arrive(cbuf.at[column(kh, 0) * 2 + 1 - core], "cpts", ("cp", kh, 0))
        arrive(hc.at[column(kh, 0) * 2 + 1 - core], "cfac", ("hp", kh, 0))
        for kl in range(1, low):
            arrive(hc.at[column(kh, kl) * 2 + 1 - core], "cfac", ("he", kh, kl))
            for c in range(cuts):
                arrive(cbuf.at[column(kh, kl) * 2 + 1 - core, part(c)], "cpts", ("ce", kh, kl, c))
        for ky in range(side):
            tile(ky, kh)

    me_c = cid * 2 + core
    mydev = row * ncol + col
    tot = None
    for kh in range(high):
        csum[me_c, at_h(kh, -1)] = col_acc[kh]
        tot = col_acc[kh] if tot is None else tot + col_acc[kh]
    tsum[mydev] = jnp.concatenate([moment, fold(tot), spread], axis=1)
    rsum[rid, side, :, :rank] = weight
    for ky in range(side):
        rsum[rid, at_y(ky, -1), :, : side * rows] = jnp.sum(row_acc[ky].T, axis=0, keepdims=True)

    def each(count, action):
        def body(k, carry):
            action(k)
            return carry

        lax.fori_loop(1, count, body, 0, unroll=count <= 32)

    def total_to(k):
        there = ((row + k // ncol) % nrow, (col + k % ncol) % ncol)
        send(tsum.at[mydev], tsum.at[mydev], "tsum", ("tsum",), there)

    each(nrow * ncol, total_to)
    for n in range(1, nr):
        send(rsum.at[rid], rsum.at[rid], "rsum", ("rsum",), in_plane(n))
    for kh in range(high):
        for kl in range(low):
            for flip in range(2):
                if kh or kl or flip:
                    there, cc = device(at_h(kh, 1), at_l(kl, 1), y, x)
                    there = there + flip * (1 - 2 * core)
                    send(csum.at[me_c], csum.at[me_c], "csum", ("csum",), (there, cc))

    def to_row_group(src, dst, kind):
        for n in range(nr - 1, 0, -1):
            send(src.at[row_peer(n, 1)], dst.at[rid], kind, (kind, n), in_plane(n))

    for ky in range(side):
        psend[pl.ds(at_y(ky, -1) * side, side)] = forces[ky].reshape(side, rows, rank)
    to_row_group(psend, precv, "pull")

    def gram_of(block):
        return lax.dot_general(block, block, (((0,), (0,)), ((), ())), preferred_element_type=jnp.float32)

    arrive(rsum.at[pl.ds(0, nr - 1)], "rsum", ("rsum",))
    arrive(csum.at[pl.ds(0, 2 * nc - 1)], "csum", ("csum",))
    arrive(tsum.at[pl.ds(0, nrow * ncol - 1)], "tsum", ("tsum",))
    sums = jnp.sum(tsum[...], axis=0)
    moment = sums[:, :rank] / total
    grand = jnp.sum(sums[:, rank : rank + 128], axis=1, keepdims=True) / (total * total)
    scale = 0.5 / jnp.sqrt(jnp.sum(sums[:, rank + 128 :], axis=1, keepdims=True) + 1e-06)
    weight = jnp.sum(rsum[:, side], axis=0)[:, :rank]
    col_mean = [jnp.sum(csum[:, i], axis=0) / total for i in range(high)]
    for j in range(side):
        row_mean = jnp.sum(rsum[:, j], axis=0)[:, : side * rows] / total
        mean_r = jnp.broadcast_to(row_mean, (128, side * rows)).T
        means[j] = mean_r
        mean_r = jnp.concatenate([mean_r] * (low * wide // 128), axis=1)
        for i in range(high):
            a = (kern[j, i] - mean_r - col_mean[i] + grand).astype(jnp.bfloat16)
            for k in range(side):
                for l in range(low):
                    asend[j * side + k, i * low + l] = a[k * rows : (k + 1) * rows, l * wide : (l + 1) * wide]
    to_row_group(asend, arecv, "aff")
    arecv[rid] = asend[rid]

    mean = jnp.concatenate([means[y, pl.ds(pl.multiple_of(x * rows, rows), rows)]] * (rank // 128), axis=1)
    centre = 1.0 - 2.0 * mean + grand
    rounding = centre.astype(jnp.bfloat16).astype(jnp.float32) - centre
    force = mean * weight + (moment - grand * weight) - rounding * hb.astype(jnp.float32) + psend[rid]
    for n in range(1, nr):
        arrive(precv.at[row_peer(n, -1)], "pull", ("pull", n))
        force += precv[row_peer(n, -1)]
    h = jnp.maximum(h - scale * force, 0.0)

    offsets = [(kh, kl) for kh in range(high) for kl in range(low)]

    def held(n, p):
        return later.at[(column(*offsets[n]) * nr + row_peer(p, -1)) * 2 + core]

    def along_z():
        for n in range(nz - 1, 0, -1):
            kh, kl = offsets[n]
            send(held(0, 0), held(0, 0), "later", ("z", n), device(at_h(kh, 1), at_l(kl, 1), y, x))

    def over_plane(n):
        block = held(n, 0)
        if n:
            arrive(block, "later", ("z", n))
        for p in range(nr - 1, 0, -1):
            send(block, block, "later", ("plane", n, p), in_plane(p))
        send(block, block, "later", ("partner", n), partner)

    def to_partner(n):
        for p in range(1, nr):
            arrive(held(n, p), "later", ("plane", n, p))
            send(held(n, p), held(n, p), "later", ("partner", n), partner)

    later[(cid * nr + rid) * 2 + core] = h.astype(jnp.bfloat16)
    along_z()
    over_plane(0)
    for n in range(1, nr):
        arrive(arecv.at[row_peer(n, -1)], "aff", ("aff", n))
    ah = jnp.zeros((rows, rank), jnp.float32)
    hh = jnp.zeros((rank, rank), jnp.float32)
    for t in range(1, nz + 2):
        if t < nz:
            over_plane(t)
        if t <= nz:
            to_partner(t - 1)
        if t >= 2:
            arrive(later.at[pl.ds(0, nr)], "later", ("partner", t - 2))
            c = column(*offsets[t - 2])
            block = later[pl.ds(c * nr * 2, nr * 2)].reshape(nr * wide, rank)
            slab = jnp.concatenate([arecv[r, c] for r in range(nr)], axis=1)
            ah += jnp.dot(slab, block, preferred_element_type=jnp.float32)
            hh += gram_of(block)
    scale = 0.5 / jnp.sqrt(jnp.sum(hh * hh, keepdims=True) + 1e-06)
    hhh = jnp.dot(h, hh, precision=lax.Precision.HIGHEST, preferred_element_type=jnp.float32)
    out_ref[...] = jnp.maximum(h - scale * (hhh - ah), 0.0) / unit

    def sent(ref, kind):
        remote(ref, ref, kind, ("tsum",), partner).wait_send()

    sent(rbuf.at[pl.ds(0, nr - 1)], "rpts")
    sent(cbuf.at[pl.ds(0, 2 * nc - 1)], "cpts")
    sent(hr.at[pl.ds(0, nr - 1)], "rfac")
    sent(hc.at[pl.ds(0, 2 * nc - 1)], "cfac")
    sent(rsum.at[pl.ds(0, nr - 1)], "rsum")
    sent(csum.at[pl.ds(0, 2 * nc - 1)], "csum")
    sent(tsum.at[pl.ds(0, nrow * ncol - 1)], "tsum")
    sent(psend.at[pl.ds(0, nr - 1)], "pull")
    sent(asend.at[pl.ds(0, nr - 1)], "aff")
    sent(later.at[pl.ds(0, nrow * ncol - 1)], "later")


def solution(mesh):
    nrow, ncol = mesh.shape["row"], mesh.shape["col"]
    side, low, high = layout(nrow, ncol)

    def shards(points, factor):
        rows, width = points.shape
        rank = factor.shape[1]
        wide = 2 * rows
        nr, nc = side * side, low * high
        keys = receive_keys(nrow, ncol, rows)
        buffers = [
            ((nr, rows, width), jnp.bfloat16),
            ((2 * nc, rows, width), jnp.bfloat16),
            ((nr, rows, rank), jnp.bfloat16),
            ((2 * nc, rows, rank), jnp.bfloat16),
            ((nrow * ncol, rows, rank), jnp.bfloat16),
            ((side, high, side * rows, low * wide), jnp.float32),
            ((nr, rows, rank), jnp.float32),
            ((nr, rows, rank), jnp.float32),
            ((nr, nc, rows, wide), jnp.bfloat16),
            ((nr, nc, rows, wide), jnp.bfloat16),
            ((side, side * rows, 128), jnp.float32),
            ((nr, side + 1, 1, max(side * rows, rank)), jnp.float32),
            ((2 * nc, high, 1, low * wide), jnp.float32),
            ((nrow * ncol, 1, rank + 256), jnp.float32),
        ]
        held = sum(math.prod(shape) * jnp.dtype(kind).itemsize for shape, kind in buffers)
        return pl.pallas_call(
            functools.partial(kernel, nrow, ncol, keys),
            out_shape=jax.ShapeDtypeStruct((rows, rank), jnp.float32),
            in_specs=[pl.BlockSpec(memory_space=pltpu.VMEM)] * 2,
            out_specs=pl.BlockSpec(memory_space=pltpu.VMEM),
            scratch_shapes=[pltpu.VMEM(shape, kind) for shape, kind in buffers]
            + [pltpu.SemaphoreType.DMA((len(SENDS),)), pltpu.SemaphoreType.DMA((len(keys),))],
            compiler_params=pltpu.CompilerParams(
                collective_id=0, has_side_effects=True, vmem_limit_bytes=min(67043328, held + (16 << 20))
            ),
        )(points, factor)

    spec = P(("row", "col"), None)
    return jax.shard_map(shards, mesh=mesh, in_specs=(spec, spec), out_specs=spec, check_vma=False)
```

```python
import functools
import math

import jax
import jax.numpy as jnp
from jax import lax
from jax.experimental import pallas as pl
from jax.experimental.pallas import tpu as pltpu
from jax.sharding import PartitionSpec as P

MESH = pl.DeviceIdType.MESH

SENDS = ("rpts", "cline", "cpart", "rfac", "hline", "hpart", "later", "rsum", "csum", "tsum", "pull", "aff")


def layout(nrow, ncol):
    return math.isqrt(ncol), nrow // 2


def cuts_of(rows):
    return 4 if rows % 64 == 0 else 1


def receive_keys(nrow, ncol, rows):
    side, nz = layout(nrow, ncol)
    cuts, plane = cuts_of(rows), side * side
    keys = [(name, k) for name in ("rx", "hx", "hy") for k in range(1, side)]
    keys += [("ry", k, c) for k in range(1, side) for c in range(cuts)]
    keys += [("rd", j, k, c) for j in range(1, side) for k in range(1, side) for c in range(cuts)]
    keys += [("hd", j, k) for j in range(1, side) for k in range(1, side)]
    keys += [("line", k) for k in range(nz * (cuts + 1))]
    keys += [("cross", k) for k in range(nz * 2)]
    keys += [("rsum",), ("csum",), ("tsum",)]
    keys += [(name, k) for name in ("aff", "pull") for k in range(1, plane)]
    keys += [("z", k) for k in range(1, nz)]
    keys += [("plane", k, p) for k in range(nz) for p in range(1, plane)]
    keys += [("partner", k) for k in range(nz)]
    return {key: i for i, key in enumerate(keys)}


def shift(i, k, n, sign):
    if n & (n - 1) or n == 2:
        return (i + sign * k + n) % n
    out, bit = i, 1
    while bit < n:
        if k & bit:
            out = out + bit - 2 * bit * ((i // bit) % 2)
        bit *= 2
    return out


def kernel(nrow, ncol, keys, pts_ref, fac_ref, out_ref, rbuf, cbuf, hr, hc, later, kern, psend, precv, asend, arecv, means, rsum, csum, tsum, ssem, rsem):
    side, nz = layout(nrow, ncol)
    rows, width = pts_ref.shape
    rank = fac_ref.shape[1]
    wide = 2 * rows
    nr = side * side
    total = rows * nrow * ncol
    unit = 2.0 / math.sqrt(total * rank)
    cuts = cuts_of(rows)
    piece = rows // cuts
    row, col = lax.axis_index("row"), lax.axis_index("col")
    z, core = row // 2, row % 2
    y, x = col // side, col % side
    rid = y * side + x
    partner = (z * 2 + 1 - core, col)

    def device(zz, yy, xx):
        return (zz * 2 + core, yy * side + xx)

    def at_z(k, sign):
        return shift(z, k, nz, sign)

    def at_y(k, sign):
        return (y + sign * k + side) % side

    def at_x(k, sign):
        return (x + sign * k + side) % side

    def remote(src, dst, kind, key, where):
        return pltpu.make_async_remote_copy(
            src_ref=src,
            dst_ref=dst,
            send_sem=ssem.at[SENDS.index(kind)],
            recv_sem=rsem.at[keys[key]],
            device_id=where,
            device_id_type=MESH,
        )

    def send(src, dst, kind, key, where):
        remote(src, dst, kind, key, where).start()

    def arrive(block, kind, key):
        remote(block, block, kind, key, partner).wait_recv()

    plane = [(ky, kx) for ky in range(side) for kx in range(side)]

    def row_peer(n, sign):
        ky, kx = plane[n]
        return at_y(ky, sign) * side + at_x(kx, sign)

    def in_plane(n):
        ky, kx = plane[n]
        return device(z, at_y(ky, 1), at_x(kx, 1))

    barrier = pltpu.get_barrier_semaphore()
    peers = [device(z, y, at_x(k, 1)) for k in range(1, side)]
    peers += [device(z, at_y(k, 1), x) for k in range(1, side)]
    peers.append(partner)
    for peer in peers:
        pl.semaphore_signal(barrier, inc=1, device_id=peer, device_id_type=MESH)
    not_low, not_high = z > 0, z < nz - 1

    @pl.when(not_low)
    def _():
        pl.semaphore_signal(barrier, inc=1, device_id=device(z - 1, y, x), device_id_type=MESH)

    @pl.when(not_high)
    def _():
        pl.semaphore_signal(barrier, inc=1, device_id=device(z + 1, y, x), device_id_type=MESH)

    h = fac_ref[...] * unit
    hb = h.astype(jnp.bfloat16)
    hr[rid] = hb
    hc[z * 2 + core] = hb
    rbuf[rid] = pts_ref[...]
    cbuf[z * 2 + core] = pts_ref[...]
    pl.semaphore_wait(barrier, len(peers) + jnp.minimum(z, 1) + jnp.minimum(nz - 1 - z, 1))

    def part(c):
        return pl.ds(c * piece, piece)

    def line_copy(src, c, where=None, local=None):
        block = hc.at[src * 2 + core] if c == cuts else cbuf.at[src * 2 + core, part(c)]
        return pltpu.make_async_remote_copy(
            src_ref=block if local is None else local,
            dst_ref=block,
            send_sem=ssem.at[SENDS.index("hline" if c == cuts else "cline")],
            recv_sem=rsem.at[keys["line", 0] + src * (cuts + 1) + c],
            device_id=partner if where is None else device(where, y, x),
            device_id_type=MESH,
        )

    def cross_copy(src, c, local=None):
        slot = src * 2 + core
        block = hc.at[slot] if c == cuts else cbuf.at[slot] if c is None else cbuf.at[slot, part(c)]
        return pltpu.make_async_remote_copy(
            src_ref=block if local is None else local,
            dst_ref=block,
            send_sem=ssem.at[SENDS.index("hpart" if c == cuts else "cpart")],
            recv_sem=rsem.at[keys["cross", 0] + src * 2 + (1 if c == cuts else 0)],
            device_id=partner,
            device_id_type=MESH,
        )

    def cross_wait(src):
        for block, k in ((cbuf.at[src * 2 + 1 - core], 0), (hc.at[src * 2 + 1 - core], 1)):
            pltpu.make_async_remote_copy(
                src_ref=block,
                dst_ref=block,
                send_sem=ssem.at[0],
                recv_sem=rsem.at[keys["cross", 0] + src * 2 + k],
                device_id=partner,
                device_id_type=MESH,
            ).wait_recv()

    def own_piece(c):
        local = None if c == cuts else pts_ref.at[part(c)]

        @pl.when(not_low)
        def _():
            line_copy(z, c, z - 1, local).start()

        @pl.when(not_high)
        def _():
            line_copy(z, c, z + 1, local).start()

    for c in range(cuts):
        own_piece(c)
        for k in range(1, side):
            send(pts_ref.at[part(c)], rbuf.at[rid, part(c)], "rpts", ("ry", k, c), device(z, at_y(k, 1), x))
    for k in range(1, side):
        send(pts_ref, rbuf.at[rid], "rpts", ("rx", k), device(z, y, at_x(k, 1)))
        send(hr.at[rid], hr.at[rid], "rfac", ("hx", k), device(z, y, at_x(k, 1)))
        send(hr.at[rid], hr.at[rid], "rfac", ("hy", k), device(z, at_y(k, 1), x))
    cross_copy(z, None, pts_ref).start()
    cross_copy(z, cuts).start()

    def pass_along(d, c):
        @pl.when(z + d < nz)
        def _():
            line_copy(z + d, c).wait_recv()

            @pl.when(not_low)
            def _():
                line_copy(z + d, c, z - 1).start()

            cross_copy(z + d, c).start()

        @pl.when(z >= d)
        def _():
            line_copy(z - d, c).wait_recv()

            @pl.when(not_high)
            def _():
                line_copy(z - d, c, z + 1).start()

            cross_copy(z - d, c).start()

    def pass_over(c):
        for k in range(1, side):
            other = at_y(k, -1) * side + x
            block = hr.at[other] if c == cuts else rbuf.at[other, part(c)]
            kind, key = ("rfac", ("hy", k)) if c == cuts else ("rpts", ("ry", k, c))
            arrive(block, kind, key)
            for kx in range(1, side):
                key = ("hd", k, kx) if c == cuts else ("rd", k, kx, c)
                send(block, block, kind, key, device(z, y, at_x(kx, 1)))

    for c in range(cuts):
        pass_over(c)
        if c == 0:
            own_piece(cuts)
        if nz > 1:
            pass_along(1, c)
    pass_over(cuts)
    if nz > 1:
        pass_along(1, cuts)
    for d in range(2, nz - 1):
        for c in range(cuts + 1):
            pass_along(d, c)

    def squares(block):
        acc = None
        for k in range(0, width, 128):
            one = block[:, k : k + 128].astype(jnp.float32)
            acc = one * one if acc is None else acc + one * one
        return acc

    tall = min(nr * rows, 256)
    bands = nr * rows // tall
    row_sq, row_acc, forces, tots = [None] * bands, [None] * bands, [None] * bands, []
    moment = jnp.zeros((1, rank), jnp.float32)
    spread = jnp.zeros((1, 128), jnp.float32)
    weight = jnp.zeros((1, rank), jnp.float32)
    me_c = z * 2 + core
    mydev = row * ncol + col

    def fold(a):
        out = a[:, :128]
        for j in range(128, a.shape[1], 128):
            out += a[:, j : j + 128]
        return out

    def split(a):
        near = a.astype(jnp.bfloat16)
        return near, (a - near.astype(jnp.float32)).astype(jnp.bfloat16)

    def plus(a, b):
        return b if a is None else a + b

    def tile(first, count):
        nonlocal moment, spread, weight
        block = cbuf[pl.ds(first * 2, count * 2)].reshape(count * wide, width)
        hcol = hc[pl.ds(first * 2, count * 2)].reshape(count * wide, rank)
        col_sq = jnp.sum(squares(block).T, axis=0, keepdims=True)
        weight += jnp.sum(hcol.astype(jnp.float32), axis=0, keepdims=True)
        below = None
        for b in range(bands):
            group = tall // rows
            mat = rbuf[b * group : (b + 1) * group].reshape(tall, width)
            hrow = hr[b * group : (b + 1) * group].reshape(tall, rank)
            if row_sq[b] is None:
                row_sq[b] = jnp.sum(squares(mat), axis=1, keepdims=True)
            inner = lax.dot_general(hrow, hcol, (((1,), (1,)), ((), ())), preferred_element_type=jnp.float32)
            spread += jnp.sum(fold(inner * inner), axis=0, keepdims=True)
            gram = lax.dot_general(mat, block, (((1,), (1,)), ((), ())), preferred_element_type=jnp.float32)
            k = jnp.exp((2.0 * gram - row_sq[b] - col_sq) * (0.5 / width))
            for i in range(count):
                kern[first + i, b * tall : (b + 1) * tall] = k[:, i * wide : (i + 1) * wide]
            left = jnp.concatenate([*split(k), *split(inner)], axis=0)
            prod = jnp.dot(left, hcol, preferred_element_type=jnp.float32)
            drawn = prod[:tall] + prod[tall : 2 * tall]
            moment += jnp.sum(drawn, axis=0, keepdims=True)
            forces[b] = plus(forces[b], prod[2 * tall : 3 * tall] + prod[3 * tall :] - drawn)
            row_acc[b] = plus(row_acc[b], fold(k))
            below = plus(below, jnp.sum(k, axis=0, keepdims=True))
        for i in range(count):
            csum[me_c, first + i] = below[:, i * wide : (i + 1) * wide]
        tots.append(fold(below))

    def nth(n):
        up = 2 * z // nz
        sign, near = 1 - 2 * up, z + up * (nz - 1 - 2 * z)
        paired = jnp.minimum(near // ((n + 1) // 2), 1)
        return z + sign * (paired * (-((n + 1) // 2) if n % 2 else n // 2) + (1 - paired) * (n - near))

    for k in range(1, side):
        arrive(rbuf.at[y * side + at_x(k, -1)], "rpts", ("rx", k))
        arrive(hr.at[y * side + at_x(k, -1)], "rfac", ("hx", k))
    for ky in range(1, side):
        for kx in range(1, side):
            other = at_y(ky, -1) * side + at_x(kx, -1)
            for c in range(cuts):
                arrive(rbuf.at[other, part(c)], "rpts", ("rd", ky, kx, c))
            arrive(hr.at[other], "rfac", ("hd", ky, kx))
    for n in range(nz):
        if n == nz - 1 and nz > 2:
            for c in range(cuts + 1):
                pass_along(n, c)
        chip = nth(n) if n else z
        cross_wait(chip)
        tile(chip, 1)

    tot = sum(tots[1:], tots[0])
    tsum[mydev] = jnp.concatenate([moment, tot, spread], axis=1)
    rsum[rid, 1, :, :rank] = weight
    for b in range(bands):
        rsum[rid, 0, :, b * tall : (b + 1) * tall] = jnp.sum(row_acc[b].T, axis=0, keepdims=True)

    def each(count, action):
        def body(k, carry):
            action(k)
            return carry

        lax.fori_loop(1, count, body, 0, unroll=count <= 32)

    def total_to(k):
        there = ((row + k // ncol) % nrow, (col + k % ncol) % ncol)
        send(tsum.at[mydev], tsum.at[mydev], "tsum", ("tsum",), there)

    each(nrow * ncol, total_to)
    for n in range(1, nr):
        send(rsum.at[rid], rsum.at[rid], "rsum", ("rsum",), in_plane(n))
    for k in range(nz):
        for flip in range(2):
            if k or flip:
                there, cc = device(at_z(k, 1), y, x)
                there = there + flip * (1 - 2 * core)
                send(csum.at[me_c], csum.at[me_c], "csum", ("csum",), (there, cc))

    def to_row_group(src, dst, kind):
        for n in range(nr - 1, 0, -1):
            send(src.at[row_peer(n, 1)], dst.at[rid], kind, (kind, n), in_plane(n))

    for b in range(bands):
        group = tall // rows
        psend[b * group : (b + 1) * group] = forces[b].reshape(group, rows, rank)
    to_row_group(psend, precv, "pull")

    def gram_of(block):
        return lax.dot_general(block, block, (((0,), (0,)), ((), ())), preferred_element_type=jnp.float32)

    arrive(rsum.at[pl.ds(0, nr - 1)], "rsum", ("rsum",))
    arrive(csum.at[pl.ds(0, 2 * nz - 1)], "csum", ("csum",))
    arrive(tsum.at[pl.ds(0, nrow * ncol - 1)], "tsum", ("tsum",))
    sums = jnp.sum(tsum[...], axis=0)
    moment = sums[:, :rank] / total
    grand = jnp.sum(sums[:, rank : rank + 128], axis=1, keepdims=True) / (total * total)
    scale = 0.5 / jnp.sqrt(jnp.sum(sums[:, rank + 128 :], axis=1, keepdims=True) + 1e-06)
    weight = jnp.sum(rsum[:, 1], axis=0)[:, :rank]
    row_mean = jnp.sum(rsum[:, 0], axis=0) / total
    col_mean = [jnp.sum(csum[:, c], axis=0) / total for c in range(nz)]
    for b in range(bands):
        mean_r = jnp.broadcast_to(row_mean[:, b * tall : (b + 1) * tall], (128, tall)).T
        means[b * tall : (b + 1) * tall] = mean_r
        for c in range(nz):
            a = (kern[c, b * tall : (b + 1) * tall] - mean_r - col_mean[c] + grand).astype(jnp.bfloat16)
            group = tall // rows
            asend[b * group : (b + 1) * group, c] = a.reshape(group, rows, wide)
    to_row_group(asend, arecv, "aff")
    arecv[rid] = asend[rid]

    mean = jnp.concatenate([means[pl.ds(pl.multiple_of(rid * rows, rows), rows)]] * (rank // 128), axis=1)
    centre = 1.0 - 2.0 * mean + grand
    rounding = centre.astype(jnp.bfloat16).astype(jnp.float32) - centre
    force = mean * weight + (moment - grand * weight) - rounding * hb.astype(jnp.float32) + psend[rid]
    for n in range(1, nr):
        arrive(precv.at[row_peer(n, -1)], "pull", ("pull", n))
        force += precv[row_peer(n, -1)]
    h = jnp.maximum(h - scale * force, 0.0)

    def held(n, p):
        return later.at[(at_z(n, -1) * nr + row_peer(p, -1)) * 2 + core]

    def along_z():
        for n in range(nz - 1, 0, -1):
            send(held(0, 0), held(0, 0), "later", ("z", n), device(at_z(n, 1), y, x))

    def over_plane(n):
        block = held(n, 0)
        if n:
            arrive(block, "later", ("z", n))
        for p in range(nr - 1, 0, -1):
            send(block, block, "later", ("plane", n, p), in_plane(p))
        send(block, block, "later", ("partner", n), partner)

    def to_partner(n):
        for p in range(1, nr):
            arrive(held(n, p), "later", ("plane", n, p))
            send(held(n, p), held(n, p), "later", ("partner", n), partner)

    later[(z * nr + rid) * 2 + core] = h.astype(jnp.bfloat16)
    along_z()
    over_plane(0)
    ah = jnp.zeros((rows, rank), jnp.float32)
    hh = jnp.zeros((rank, rank), jnp.float32)
    for t in range(1, nz + 2):
        if t < nz:
            over_plane(t)
        if t <= nz:
            to_partner(t - 1)
        if t >= 2:
            if t == 2:
                for n in range(1, nr):
                    arrive(arecv.at[row_peer(n, -1)], "aff", ("aff", n))
            arrive(later.at[pl.ds(0, nr)], "later", ("partner", t - 2))
            c = at_z(t - 2, -1)
            block = later[pl.ds(c * nr * 2, nr * 2)].reshape(nr * wide, rank)
            slab = jnp.concatenate([arecv[r, c] for r in range(nr)], axis=1)
            ah += jnp.dot(slab, block, preferred_element_type=jnp.float32)
            hh += gram_of(block)
    scale = 0.5 / jnp.sqrt(jnp.sum(hh * hh, keepdims=True) + 1e-06)
    hhh = jnp.dot(h, hh, precision=lax.Precision.HIGHEST, preferred_element_type=jnp.float32)
    out_ref[...] = jnp.maximum(h - scale * (hhh - ah), 0.0) / unit

    def sent(ref, kind):
        remote(ref, ref, kind, ("tsum",), partner).wait_send()

    sent(rbuf.at[pl.ds(0, nr - 1)], "rpts")
    sent(hr.at[pl.ds(0, nr - 1)], "rfac")
    sent(cbuf.at[pl.ds(0, nz)], "cpart")
    sent(hc.at[pl.ds(0, nz)], "hpart")
    ends = (z + nz - 1) % nz >= nz - 2
    if nz > 1:

        @pl.when(ends)
        def _():
            sent(cbuf.at[pl.ds(0, 1)], "cline")
            sent(hc.at[pl.ds(0, 1)], "hline")

    if nz > 2:

        @pl.when(jnp.logical_not(ends))
        def _():
            sent(cbuf.at[pl.ds(0, nz + 1)], "cline")
            sent(hc.at[pl.ds(0, nz + 1)], "hline")

    sent(rsum.at[pl.ds(0, nr - 1)], "rsum")
    sent(csum.at[pl.ds(0, 2 * nz - 1)], "csum")
    sent(tsum.at[pl.ds(0, nrow * ncol - 1)], "tsum")
    sent(psend.at[pl.ds(0, nr - 1)], "pull")
    sent(asend.at[pl.ds(0, nr - 1)], "aff")
    sent(later.at[pl.ds(0, nrow * ncol - 1)], "later")


def solution(mesh):
    nrow, ncol = mesh.shape["row"], mesh.shape["col"]
    side, nz = layout(nrow, ncol)

    def shards(points, factor):
        rows, width = points.shape
        rank = factor.shape[1]
        wide = 2 * rows
        nr = side * side
        keys = receive_keys(nrow, ncol, rows)
        buffers = [
            ((nr, rows, width), jnp.bfloat16),
            ((2 * nz, rows, width), jnp.bfloat16),
            ((nr, rows, rank), jnp.bfloat16),
            ((2 * nz, rows, rank), jnp.bfloat16),
            ((nrow * ncol, rows, rank), jnp.bfloat16),
            ((nz, nr * rows, wide), jnp.float32),
            ((nr, rows, rank), jnp.float32),
            ((nr, rows, rank), jnp.float32),
            ((nr, nz, rows, wide), jnp.bfloat16),
            ((nr, nz, rows, wide), jnp.bfloat16),
            ((nr * rows, 128), jnp.float32),
            ((nr, 2, 1, max(nr * rows, rank)), jnp.float32),
            ((2 * nz, nz, 1, wide), jnp.float32),
            ((nrow * ncol, 1, rank + 256), jnp.float32),
        ]
        held = sum(math.prod(shape) * jnp.dtype(kind).itemsize for shape, kind in buffers)
        return pl.pallas_call(
            functools.partial(kernel, nrow, ncol, keys),
            out_shape=jax.ShapeDtypeStruct((rows, rank), jnp.float32),
            in_specs=[pl.BlockSpec(memory_space=pltpu.VMEM)] * 2,
            out_specs=pl.BlockSpec(memory_space=pltpu.VMEM),
            scratch_shapes=[pltpu.VMEM(shape, kind) for shape, kind in buffers]
            + [pltpu.SemaphoreType.DMA((len(SENDS),)), pltpu.SemaphoreType.DMA((len(keys),))],
            compiler_params=pltpu.CompilerParams(
                collective_id=0, has_side_effects=True, vmem_limit_bytes=min(67043328, held + (16 << 20))
            ),
        )(points, factor)

    spec = P(("row", "col"), None)
    return jax.shard_map(shards, mesh=mesh, in_specs=(spec, spec), out_specs=spec, check_vma=False)
```

```python
import functools
import math

import jax
import jax.numpy as jnp
from jax import lax
from jax.experimental import pallas as pl
from jax.experimental.pallas import tpu as pltpu
from jax.sharding import PartitionSpec as P

MESH = pl.DeviceIdType.MESH

SENDS = ("rpts", "cline", "cpart", "rfac", "hline", "hpart", "later", "rsum", "csum", "tsum", "pull", "aff")


def layout(nrow, ncol):
    return math.isqrt(ncol), nrow // 2


def cuts_of(rows):
    return 4 if rows % 64 == 0 else 1


def receive_keys(nrow, ncol, rows):
    side, nz = layout(nrow, ncol)
    cuts, plane = cuts_of(rows), side * side
    keys = [(name, k) for name in ("rx", "hx", "hy") for k in range(1, side)]
    keys += [("ry", k, c) for k in range(1, side) for c in range(cuts)]
    keys += [("rd", j, k, c) for j in range(1, side) for k in range(1, side) for c in range(cuts)]
    keys += [("hd", j, k) for j in range(1, side) for k in range(1, side)]
    keys += [("line", k) for k in range(nz * (cuts + 1))]
    keys += [("cross", k) for k in range(nz * 2)]
    keys += [("rsum",), ("csum",), ("tsum",)]
    keys += [(name, k) for name in ("aff", "pull") for k in range(1, plane)]
    keys += [("z", k) for k in range(1, nz)]
    keys += [("plane", k, p) for k in range(nz) for p in range(1, plane)]
    keys += [("partner", k) for k in range(nz)]
    return {key: i for i, key in enumerate(keys)}


def shift(i, k, n, sign):
    if n & (n - 1) or n == 2:
        return (i + sign * k + n) % n
    out, bit = i, 1
    while bit < n:
        if k & bit:
            out = out + bit - 2 * bit * ((i // bit) % 2)
        bit *= 2
    return out


def kernel(nrow, ncol, keys, pts_ref, fac_ref, out_ref, rbuf, cbuf, hr, hc, later, kern, psend, precv, asend, arecv, means, rsum, csum, tsum, ssem, rsem):
    side, nz = layout(nrow, ncol)
    rows, width = pts_ref.shape
    rank = fac_ref.shape[1]
    wide = 2 * rows
    nr = side * side
    total = rows * nrow * ncol
    unit = 2.0 / math.sqrt(total * rank)
    cuts = cuts_of(rows)
    piece = rows // cuts
    row, col = lax.axis_index("row"), lax.axis_index("col")
    z, core = row // 2, row % 2
    y, x = col // side, col % side
    rid = y * side + x
    partner = (z * 2 + 1 - core, col)

    def device(zz, yy, xx):
        return (zz * 2 + core, yy * side + xx)

    def at_z(k, sign):
        return shift(z, k, nz, sign)

    def at_y(k, sign):
        return (y + sign * k + side) % side

    def at_x(k, sign):
        return (x + sign * k + side) % side

    def remote(src, dst, kind, key, where):
        return pltpu.make_async_remote_copy(
            src_ref=src,
            dst_ref=dst,
            send_sem=ssem.at[SENDS.index(kind)],
            recv_sem=rsem.at[keys[key]],
            device_id=where,
            device_id_type=MESH,
        )

    def send(src, dst, kind, key, where):
        remote(src, dst, kind, key, where).start()

    def arrive(block, kind, key):
        remote(block, block, kind, key, partner).wait_recv()

    plane = [(ky, kx) for ky in range(side) for kx in range(side)]

    def row_peer(n, sign):
        ky, kx = plane[n]
        return at_y(ky, sign) * side + at_x(kx, sign)

    def in_plane(n):
        ky, kx = plane[n]
        return device(z, at_y(ky, 1), at_x(kx, 1))

    barrier = pltpu.get_barrier_semaphore()
    peers = [device(z, y, at_x(k, 1)) for k in range(1, side)]
    peers += [device(z, at_y(k, 1), x) for k in range(1, side)]
    peers.append(partner)
    for peer in peers:
        pl.semaphore_signal(barrier, inc=1, device_id=peer, device_id_type=MESH)
    not_low, not_high = z > 0, z < nz - 1

    @pl.when(not_low)
    def _():
        pl.semaphore_signal(barrier, inc=1, device_id=device(z - 1, y, x), device_id_type=MESH)

    @pl.when(not_high)
    def _():
        pl.semaphore_signal(barrier, inc=1, device_id=device(z + 1, y, x), device_id_type=MESH)

    h = fac_ref[...] * unit
    hb = h.astype(jnp.bfloat16)
    hr[rid] = hb
    hc[z * 2 + core] = hb
    rbuf[rid] = pts_ref[...]
    cbuf[z * 2 + core] = pts_ref[...]
    pl.semaphore_wait(barrier, len(peers) + jnp.minimum(z, 1) + jnp.minimum(nz - 1 - z, 1))

    def part(c):
        return pl.ds(c * piece, piece)

    def line_copy(src, c, where=None, local=None):
        block = hc.at[src * 2 + core] if c == cuts else cbuf.at[src * 2 + core, part(c)]
        return pltpu.make_async_remote_copy(
            src_ref=block if local is None else local,
            dst_ref=block,
            send_sem=ssem.at[SENDS.index("hline" if c == cuts else "cline")],
            recv_sem=rsem.at[keys["line", 0] + src * (cuts + 1) + c],
            device_id=partner if where is None else device(where, y, x),
            device_id_type=MESH,
        )

    def cross_copy(src, c, local=None):
        slot = src * 2 + core
        block = hc.at[slot] if c == cuts else cbuf.at[slot] if c is None else cbuf.at[slot, part(c)]
        return pltpu.make_async_remote_copy(
            src_ref=block if local is None else local,
            dst_ref=block,
            send_sem=ssem.at[SENDS.index("hpart" if c == cuts else "cpart")],
            recv_sem=rsem.at[keys["cross", 0] + src * 2 + (1 if c == cuts else 0)],
            device_id=partner,
            device_id_type=MESH,
        )

    def cross_wait(src):
        for block, k in ((cbuf.at[src * 2 + 1 - core], 0), (hc.at[src * 2 + 1 - core], 1)):
            pltpu.make_async_remote_copy(
                src_ref=block,
                dst_ref=block,
                send_sem=ssem.at[0],
                recv_sem=rsem.at[keys["cross", 0] + src * 2 + k],
                device_id=partner,
                device_id_type=MESH,
            ).wait_recv()

    def own_piece(c):
        local = None if c == cuts else pts_ref.at[part(c)]

        @pl.when(not_low)
        def _():
            line_copy(z, c, z - 1, local).start()

        @pl.when(not_high)
        def _():
            line_copy(z, c, z + 1, local).start()

    order = [cuts, *range(cuts)]
    for c in order[:-1]:
        own_piece(c)
    for k in range(1, side):
        send(hr.at[rid], hr.at[rid], "rfac", ("hy", k), device(z, at_y(k, 1), x))
        send(hr.at[rid], hr.at[rid], "rfac", ("hx", k), device(z, y, at_x(k, 1)))
    for c in range(cuts):
        for k in range(1, side):
            send(pts_ref.at[part(c)], rbuf.at[rid, part(c)], "rpts", ("ry", k, c), device(z, at_y(k, 1), x))
    for k in range(1, side):
        send(pts_ref, rbuf.at[rid], "rpts", ("rx", k), device(z, y, at_x(k, 1)))
    cross_copy(z, None, pts_ref).start()
    cross_copy(z, cuts).start()

    def pass_along(d, c):
        @pl.when(z + d < nz)
        def _():
            line_copy(z + d, c).wait_recv()

            @pl.when(not_low)
            def _():
                line_copy(z + d, c, z - 1).start()

            cross_copy(z + d, c).start()

        @pl.when(z >= d)
        def _():
            line_copy(z - d, c).wait_recv()

            @pl.when(not_high)
            def _():
                line_copy(z - d, c, z + 1).start()

            cross_copy(z - d, c).start()

    def pass_over(c):
        for k in range(1, side):
            other = at_y(k, -1) * side + x
            block = hr.at[other] if c == cuts else rbuf.at[other, part(c)]
            kind, key = ("rfac", ("hy", k)) if c == cuts else ("rpts", ("ry", k, c))
            arrive(block, kind, key)
            for kx in range(1, side):
                key = ("hd", k, kx) if c == cuts else ("rd", k, kx, c)
                send(block, block, kind, key, device(z, y, at_x(kx, 1)))

    for c in order:
        pass_over(c)
        if c == cuts:
            own_piece(order[-1])
        if nz > 1:
            pass_along(1, c)
    for d in range(2, nz - 1):
        for c in order:
            pass_along(d, c)

    def squares(block):
        acc = None
        for k in range(0, width, 128):
            one = block[:, k : k + 128].astype(jnp.float32)
            acc = one * one if acc is None else acc + one * one
        return acc

    tall = min(nr * rows, 256)
    bands = nr * rows // tall
    row_sq, row_acc, forces, tots = [None] * bands, [None] * bands, [None] * bands, []
    moment = jnp.zeros((1, rank), jnp.float32)
    spread = jnp.zeros((1, 128), jnp.float32)
    weight = jnp.zeros((1, rank), jnp.float32)
    me_c = z * 2 + core
    mydev = row * ncol + col

    def fold(a):
        out = a[:, :128]
        for j in range(128, a.shape[1], 128):
            out += a[:, j : j + 128]
        return out

    def split(a):
        near = a.astype(jnp.bfloat16)
        return near, (a - near.astype(jnp.float32)).astype(jnp.bfloat16)

    def plus(a, b):
        return b if a is None else a + b

    def tile(first, count):
        nonlocal moment, spread, weight
        block = cbuf[pl.ds(first * 2, count * 2)].reshape(count * wide, width)
        hcol = hc[pl.ds(first * 2, count * 2)].reshape(count * wide, rank)
        col_sq = jnp.sum(squares(block).T, axis=0, keepdims=True)
        weight += jnp.sum(hcol.astype(jnp.float32), axis=0, keepdims=True)
        below = None
        for b in range(bands):
            group = tall // rows
            mat = rbuf[b * group : (b + 1) * group].reshape(tall, width)
            hrow = hr[b * group : (b + 1) * group].reshape(tall, rank)
            if row_sq[b] is None:
                row_sq[b] = jnp.sum(squares(mat), axis=1, keepdims=True)
            inner = lax.dot_general(hrow, hcol, (((1,), (1,)), ((), ())), preferred_element_type=jnp.float32)
            spread += jnp.sum(fold(inner * inner), axis=0, keepdims=True)
            gram = lax.dot_general(mat, block, (((1,), (1,)), ((), ())), preferred_element_type=jnp.float32)
            k = jnp.exp((2.0 * gram - row_sq[b] - col_sq) * (0.5 / width))
            for i in range(count):
                kern[first + i, b * tall : (b + 1) * tall] = k[:, i * wide : (i + 1) * wide]
            left = jnp.concatenate([*split(k), *split(inner)], axis=0)
            prod = jnp.dot(left, hcol, preferred_element_type=jnp.float32)
            drawn = prod[:tall] + prod[tall : 2 * tall]
            moment += jnp.sum(drawn, axis=0, keepdims=True)
            forces[b] = plus(forces[b], prod[2 * tall : 3 * tall] + prod[3 * tall :] - drawn)
            row_acc[b] = plus(row_acc[b], fold(k))
            below = plus(below, jnp.sum(k, axis=0, keepdims=True))
        for i in range(count):
            csum[me_c, first + i] = below[:, i * wide : (i + 1) * wide]
        tots.append(fold(below))

    def nth(n):
        up = 2 * z // nz
        sign, near = 1 - 2 * up, z + up * (nz - 1 - 2 * z)
        paired = jnp.minimum(near // ((n + 1) // 2), 1)
        return z + sign * (paired * (-((n + 1) // 2) if n % 2 else n // 2) + (1 - paired) * (n - near))

    for k in range(1, side):
        arrive(rbuf.at[y * side + at_x(k, -1)], "rpts", ("rx", k))
        arrive(hr.at[y * side + at_x(k, -1)], "rfac", ("hx", k))
    for ky in range(1, side):
        for kx in range(1, side):
            other = at_y(ky, -1) * side + at_x(kx, -1)
            for c in range(cuts):
                arrive(rbuf.at[other, part(c)], "rpts", ("rd", ky, kx, c))
            arrive(hr.at[other], "rfac", ("hd", ky, kx))
    for n in range(nz):
        if n == nz - 1 and nz > 2:
            for c in order:
                pass_along(n, c)
        chip = nth(n) if n else z
        cross_wait(chip)
        tile(chip, 1)

    tot = sum(tots[1:], tots[0])
    both = [jnp.broadcast_to(jnp.sum(one, axis=1, keepdims=True), (1, 128)) for one in (tot, spread)]
    first_half = lax.broadcasted_iota(jnp.int32, (1, 128), 1) < 64
    tsum[mydev] = jnp.concatenate([moment, jnp.where(first_half, both[0], both[1])], axis=1)
    rsum[rid, 1, :, :rank] = weight
    for b in range(bands):
        rsum[rid, 0, :, b * tall : (b + 1) * tall] = jnp.sum(row_acc[b].T, axis=0, keepdims=True)

    def each(count, action):
        def body(k, carry):
            action(k)
            return carry

        lax.fori_loop(1, count, body, 0, unroll=count <= 32)

    def total_to(k):
        there = ((row + k // ncol) % nrow, (col + k % ncol) % ncol)
        send(tsum.at[mydev], tsum.at[mydev], "tsum", ("tsum",), there)

    each(nrow * ncol, total_to)
    for n in range(1, nr):
        send(rsum.at[rid], rsum.at[rid], "rsum", ("rsum",), in_plane(n))
    for k in range(nz):
        for flip in range(2):
            if k or flip:
                there, cc = device(at_z(k, 1), y, x)
                there = there + flip * (1 - 2 * core)
                send(csum.at[me_c], csum.at[me_c], "csum", ("csum",), (there, cc))

    def to_row_group(src, dst, kind):
        for n in range(nr - 1, 0, -1):
            send(src.at[row_peer(n, 1)], dst.at[rid], kind, (kind, n), in_plane(n))

    for b in range(bands):
        group = tall // rows
        psend[b * group : (b + 1) * group] = forces[b].reshape(group, rows, rank)
    to_row_group(psend, precv, "pull")

    def gram_of(block):
        return lax.dot_general(block, block, (((0,), (0,)), ((), ())), preferred_element_type=jnp.float32)

    arrive(rsum.at[pl.ds(0, nr - 1)], "rsum", ("rsum",))
    arrive(csum.at[pl.ds(0, 2 * nz - 1)], "csum", ("csum",))
    arrive(tsum.at[pl.ds(0, nrow * ncol - 1)], "tsum", ("tsum",))
    sums = jnp.sum(tsum[...], axis=0)
    moment = sums[:, :rank] / total
    grand = sums[:, rank : rank + 1] / (total * total)
    scale = 0.5 / jnp.sqrt(sums[:, rank + 64 : rank + 65] + 1e-06)
    weight = jnp.sum(rsum[:, 1], axis=0)[:, :rank]
    row_mean = jnp.sum(rsum[:, 0], axis=0) / total
    col_mean = [jnp.sum(csum[:, c], axis=0) / total for c in range(nz)]
    for b in range(bands):
        mean_r = jnp.broadcast_to(row_mean[:, b * tall : (b + 1) * tall], (128, tall)).T
        means[b * tall : (b + 1) * tall] = mean_r
        for c in range(nz):
            a = (kern[c, b * tall : (b + 1) * tall] - mean_r - col_mean[c] + grand).astype(jnp.bfloat16)
            group = tall // rows
            asend[b * group : (b + 1) * group, c] = a.reshape(group, rows, wide)
    to_row_group(asend, arecv, "aff")
    arecv[rid] = asend[rid]

    mean = jnp.concatenate([means[pl.ds(pl.multiple_of(rid * rows, rows), rows)]] * (rank // 128), axis=1)
    centre = 1.0 - 2.0 * mean + grand
    rounding = centre.astype(jnp.bfloat16).astype(jnp.float32) - centre
    force = mean * weight + (moment - grand * weight) - rounding * hb.astype(jnp.float32) + psend[rid]
    for n in range(1, nr):
        arrive(precv.at[row_peer(n, -1)], "pull", ("pull", n))
        force += precv[row_peer(n, -1)]
    h = jnp.maximum(h - scale * force, 0.0)

    def held(n, p):
        return later.at[(at_z(n, -1) * nr + row_peer(p, -1)) * 2 + core]

    def along_z():
        for n in range(nz - 1, 0, -1):
            send(held(0, 0), held(0, 0), "later", ("z", n), device(at_z(n, 1), y, x))

    def over_plane(n):
        block = held(n, 0)
        if n:
            arrive(block, "later", ("z", n))
        for p in range(nr - 1, 0, -1):
            if n != 1:
                send(block, block, "later", ("plane", n, p), in_plane(p))
        send(block, block, "later", ("partner", n), partner)

    def to_partner(n):
        for p in range(1, nr):
            arrive(held(n, p), "later", ("plane", n, p))
            if n == 0 and nz > 1:
                send(held(0, p), held(0, p), "later", ("plane", 1, p), device(at_z(1, 1), y, x))
            send(held(n, p), held(n, p), "later", ("partner", n), partner)

    later[(z * nr + rid) * 2 + core] = h.astype(jnp.bfloat16)
    along_z()
    over_plane(0)
    ah = jnp.zeros((rows, rank), jnp.float32)
    hh = jnp.zeros((rank, rank), jnp.float32)

    def use(n):
        nonlocal ah, hh
        arrive(later.at[pl.ds(0, nr)], "later", ("partner", n))
        c = at_z(n, -1)
        block = later[pl.ds(c * nr * 2, nr * 2)].reshape(nr * wide, rank)
        slab = jnp.concatenate([arecv[r, c] for r in range(nr)], axis=1)
        ah += jnp.dot(slab, block, preferred_element_type=jnp.float32)
        hh += gram_of(block)

    if nz > 1:
        over_plane(1)
    to_partner(0)
    for n in range(2, nz):
        over_plane(n)
    for n in range(1, nr):
        arrive(arecv.at[row_peer(n, -1)], "aff", ("aff", n))
    use(0)
    for n in range(1, nz):
        to_partner(n)
        if n > 1:
            use(n - 1)
    if nz > 1:
        use(nz - 1)
    scale = 0.5 / jnp.sqrt(jnp.sum(hh * hh, keepdims=True) + 1e-06)
    h_near, h_rest = split(h)
    hh_near, hh_rest = split(hh)
    hhh = jnp.dot(jnp.concatenate([h_near, h_rest], axis=0), hh_near, preferred_element_type=jnp.float32)
    hhh = hhh[:rows] + hhh[rows:] + jnp.dot(h_near, hh_rest, preferred_element_type=jnp.float32)
    out_ref[...] = jnp.maximum(h - scale * (hhh - ah), 0.0) / unit

    def sent(ref, kind):
        remote(ref, ref, kind, ("tsum",), partner).wait_send()

    sent(rbuf.at[pl.ds(0, nr - 1)], "rpts")
    sent(hr.at[pl.ds(0, nr - 1)], "rfac")
    sent(cbuf.at[pl.ds(0, nz)], "cpart")
    sent(hc.at[pl.ds(0, nz)], "hpart")
    ends = (z + nz - 1) % nz >= nz - 2
    if nz > 1:

        @pl.when(ends)
        def _():
            sent(cbuf.at[pl.ds(0, 1)], "cline")
            sent(hc.at[pl.ds(0, 1)], "hline")

    if nz > 2:

        @pl.when(jnp.logical_not(ends))
        def _():
            sent(cbuf.at[pl.ds(0, nz + 1)], "cline")
            sent(hc.at[pl.ds(0, nz + 1)], "hline")

    sent(rsum.at[pl.ds(0, nr - 1)], "rsum")
    sent(csum.at[pl.ds(0, 2 * nz - 1)], "csum")
    sent(tsum.at[pl.ds(0, nrow * ncol - 1)], "tsum")
    sent(psend.at[pl.ds(0, nr - 1)], "pull")
    sent(asend.at[pl.ds(0, nr - 1)], "aff")
    sent(later.at[pl.ds(0, nrow * ncol - 1)], "later")


def solution(mesh):
    nrow, ncol = mesh.shape["row"], mesh.shape["col"]
    side, nz = layout(nrow, ncol)

    def shards(points, factor):
        rows, width = points.shape
        rank = factor.shape[1]
        wide = 2 * rows
        nr = side * side
        keys = receive_keys(nrow, ncol, rows)
        buffers = [
            ((nr, rows, width), jnp.bfloat16),
            ((2 * nz, rows, width), jnp.bfloat16),
            ((nr, rows, rank), jnp.bfloat16),
            ((2 * nz, rows, rank), jnp.bfloat16),
            ((nrow * ncol, rows, rank), jnp.bfloat16),
            ((nz, nr * rows, wide), jnp.float32),
            ((nr, rows, rank), jnp.float32),
            ((nr, rows, rank), jnp.float32),
            ((nr, nz, rows, wide), jnp.bfloat16),
            ((nr, nz, rows, wide), jnp.bfloat16),
            ((nr * rows, 128), jnp.float32),
            ((nr, 2, 1, max(nr * rows, rank)), jnp.float32),
            ((2 * nz, nz, 1, wide), jnp.float32),
            ((nrow * ncol, 1, rank + 128), jnp.float32),
        ]
        held = sum(math.prod(shape) * jnp.dtype(kind).itemsize for shape, kind in buffers)
        return pl.pallas_call(
            functools.partial(kernel, nrow, ncol, keys),
            out_shape=jax.ShapeDtypeStruct((rows, rank), jnp.float32),
            in_specs=[pl.BlockSpec(memory_space=pltpu.VMEM)] * 2,
            out_specs=pl.BlockSpec(memory_space=pltpu.VMEM),
            scratch_shapes=[pltpu.VMEM(shape, kind) for shape, kind in buffers]
            + [pltpu.SemaphoreType.DMA((len(SENDS),)), pltpu.SemaphoreType.DMA((len(keys),))],
            compiler_params=pltpu.CompilerParams(
                collective_id=0, has_side_effects=True, vmem_limit_bytes=min(67043328, held + (16 << 20))
            ),
        )(points, factor)

    spec = P(("row", "col"), None)
    return jax.shard_map(shards, mesh=mesh, in_specs=(spec, spec), out_specs=spec, check_vma=False)
```

```python
import functools
import math

import jax
import jax.numpy as jnp
from jax import lax
from jax.experimental import pallas as pl
from jax.experimental.pallas import tpu as pltpu
from jax.sharding import PartitionSpec as P

MESH = pl.DeviceIdType.MESH

SENDS = ("rpts", "cline", "cpart", "rfac", "hline", "hpart", "later", "rsum", "csum", "tsum", "pull", "kern")


def layout(nrow, ncol):
    return math.isqrt(ncol), nrow // 2


def cuts_of(rows):
    return 4 if rows % 64 == 0 else 1


def receive_keys(nrow, ncol, rows):
    side, nz = layout(nrow, ncol)
    cuts, plane = cuts_of(rows), side * side
    keys = [(name, k) for name in ("rx", "hx", "hy") for k in range(1, side)]
    keys += [("ry", k, c) for k in range(1, side) for c in range(cuts)]
    keys += [("rd", j, k, c) for j in range(1, side) for k in range(1, side) for c in range(cuts)]
    keys += [("hd", j, k) for j in range(1, side) for k in range(1, side)]
    keys += [("line", k) for k in range(nz * (cuts + 1))]
    keys += [("cross", k) for k in range(nz * 2)]
    keys += [("rsum",), ("csum",), ("tsum",)]
    keys += [(name, k) for name in ("kern", "pull") for k in range(1, plane)]
    keys += [("z", k) for k in range(1, nz)]
    keys += [("plane", k, p) for k in range(nz) for p in range(1, plane)]
    keys += [("partner", k) for k in range(nz)]
    return {key: i for i, key in enumerate(keys)}


def line_order(z, nz, n, least):
    if not n:
        return z
    up = 2 * z // nz
    sign, near = 1 - 2 * up, z + up * (nz - 1 - 2 * z)
    paired = least(near // ((n + 1) // 2), 1)
    return z + sign * (paired * (-((n + 1) // 2) if n % 2 else n // 2) + (1 - paired) * (n - near))


def shift(i, k, n, sign):
    if n & (n - 1) or n == 2:
        return (i + sign * k + n) % n
    out, bit = i, 1
    while bit < n:
        if k & bit:
            out = out + bit - 2 * bit * ((i // bit) % 2)
        bit *= 2
    return out


def kernel(nrow, ncol, keys, pts_ref, fac_ref, out_ref, rbuf, cbuf, hr, hc, later, ksend, krecv, psend, precv, aff, means, rsum, csum, tsum, ssem, rsem):
    side, nz = layout(nrow, ncol)
    rows, width = pts_ref.shape
    rank = fac_ref.shape[1]
    wide = 2 * rows
    nr = side * side
    total = rows * nrow * ncol
    unit = 2.0 / math.sqrt(total * rank)
    cuts = cuts_of(rows)
    piece = rows // cuts
    row, col = lax.axis_index("row"), lax.axis_index("col")
    z, core = row // 2, row % 2
    y, x = col // side, col % side
    rid = y * side + x
    partner = (z * 2 + 1 - core, col)

    def device(zz, yy, xx):
        return (zz * 2 + core, yy * side + xx)

    def at_z(k, sign):
        return shift(z, k, nz, sign)

    def at_y(k, sign):
        return (y + sign * k + side) % side

    def at_x(k, sign):
        return (x + sign * k + side) % side

    def remote(src, dst, kind, key, where):
        return pltpu.make_async_remote_copy(
            src_ref=src,
            dst_ref=dst,
            send_sem=ssem.at[SENDS.index(kind)],
            recv_sem=rsem.at[keys[key]],
            device_id=where,
            device_id_type=MESH,
        )

    def send(src, dst, kind, key, where):
        remote(src, dst, kind, key, where).start()

    def arrive(block, kind, key):
        remote(block, block, kind, key, partner).wait_recv()

    plane = [(ky, kx) for ky in range(side) for kx in range(side)]

    def row_peer(n, sign):
        ky, kx = plane[n]
        return at_y(ky, sign) * side + at_x(kx, sign)

    def in_plane(n):
        ky, kx = plane[n]
        return device(z, at_y(ky, 1), at_x(kx, 1))

    barrier = pltpu.get_barrier_semaphore()
    peers = [device(z, y, at_x(k, 1)) for k in range(1, side)]
    peers += [device(z, at_y(k, 1), x) for k in range(1, side)]
    peers.append(partner)
    for peer in peers:
        pl.semaphore_signal(barrier, inc=1, device_id=peer, device_id_type=MESH)
    not_low, not_high = z > 0, z < nz - 1

    @pl.when(not_low)
    def _():
        pl.semaphore_signal(barrier, inc=1, device_id=device(z - 1, y, x), device_id_type=MESH)

    @pl.when(not_high)
    def _():
        pl.semaphore_signal(barrier, inc=1, device_id=device(z + 1, y, x), device_id_type=MESH)

    h = fac_ref[...] * unit
    hb = h.astype(jnp.bfloat16)
    hr[rid] = hb
    hc[z * 2 + core] = hb
    rbuf[rid] = pts_ref[...]
    cbuf[z * 2 + core] = pts_ref[...]
    pl.semaphore_wait(barrier, len(peers) + jnp.minimum(z, 1) + jnp.minimum(nz - 1 - z, 1))

    def part(c):
        return pl.ds(c * piece, piece)

    def line_copy(src, c, where=None, local=None):
        block = hc.at[src * 2 + core] if c == cuts else cbuf.at[src * 2 + core, part(c)]
        return pltpu.make_async_remote_copy(
            src_ref=block if local is None else local,
            dst_ref=block,
            send_sem=ssem.at[SENDS.index("hline" if c == cuts else "cline")],
            recv_sem=rsem.at[keys["line", 0] + src * (cuts + 1) + c],
            device_id=partner if where is None else device(where, y, x),
            device_id_type=MESH,
        )

    def cross_copy(src, c, local=None):
        slot = src * 2 + core
        block = hc.at[slot] if c == cuts else cbuf.at[slot] if c is None else cbuf.at[slot, part(c)]
        return pltpu.make_async_remote_copy(
            src_ref=block if local is None else local,
            dst_ref=block,
            send_sem=ssem.at[SENDS.index("hpart" if c == cuts else "cpart")],
            recv_sem=rsem.at[keys["cross", 0] + src * 2 + (1 if c == cuts else 0)],
            device_id=partner,
            device_id_type=MESH,
        )

    def cross_wait(src):
        for block, k in ((cbuf.at[src * 2 + 1 - core], 0), (hc.at[src * 2 + 1 - core], 1)):
            pltpu.make_async_remote_copy(
                src_ref=block,
                dst_ref=block,
                send_sem=ssem.at[0],
                recv_sem=rsem.at[keys["cross", 0] + src * 2 + k],
                device_id=partner,
                device_id_type=MESH,
            ).wait_recv()

    def own_piece(c):
        local = None if c == cuts else pts_ref.at[part(c)]

        @pl.when(not_low)
        def _():
            line_copy(z, c, z - 1, local).start()

        @pl.when(not_high)
        def _():
            line_copy(z, c, z + 1, local).start()

    order = [cuts, *range(cuts)]
    for c in order[:-1]:
        own_piece(c)
    for k in range(1, side):
        send(hr.at[rid], hr.at[rid], "rfac", ("hy", k), device(z, at_y(k, 1), x))
        send(hr.at[rid], hr.at[rid], "rfac", ("hx", k), device(z, y, at_x(k, 1)))
    for c in range(cuts):
        for k in range(1, side):
            send(pts_ref.at[part(c)], rbuf.at[rid, part(c)], "rpts", ("ry", k, c), device(z, at_y(k, 1), x))
    for k in range(1, side):
        send(pts_ref, rbuf.at[rid], "rpts", ("rx", k), device(z, y, at_x(k, 1)))
    cross_copy(z, None, pts_ref).start()
    cross_copy(z, cuts).start()

    def pass_along(d, c):
        @pl.when(z + d < nz)
        def _():
            line_copy(z + d, c).wait_recv()

            @pl.when(not_low)
            def _():
                line_copy(z + d, c, z - 1).start()

            cross_copy(z + d, c).start()

        @pl.when(z >= d)
        def _():
            line_copy(z - d, c).wait_recv()

            @pl.when(not_high)
            def _():
                line_copy(z - d, c, z + 1).start()

            cross_copy(z - d, c).start()

    def pass_over(c):
        for k in range(1, side):
            other = at_y(k, -1) * side + x
            block = hr.at[other] if c == cuts else rbuf.at[other, part(c)]
            kind, key = ("rfac", ("hy", k)) if c == cuts else ("rpts", ("ry", k, c))
            arrive(block, kind, key)
            for kx in range(1, side):
                key = ("hd", k, kx) if c == cuts else ("rd", k, kx, c)
                send(block, block, kind, key, device(z, y, at_x(kx, 1)))

    for c in order:
        pass_over(c)
        if c == cuts:
            own_piece(order[-1])
        if nz > 1:
            pass_along(1, c)
    for d in range(2, nz - 1):
        for c in order:
            pass_along(d, c)

    def squares(block):
        acc = None
        for k in range(0, width, 128):
            one = block[:, k : k + 128].astype(jnp.float32)
            acc = one * one if acc is None else acc + one * one
        return acc

    tall = min(nr * rows, 256)
    bands, group = nr * rows // tall, tall // rows
    row_sq, row_acc, forces, tots = [None] * bands, [None] * bands, [None] * bands, []
    moment = jnp.zeros((1, rank), jnp.float32)
    spread = jnp.zeros((1, 128), jnp.float32)
    weight = jnp.zeros((1, rank), jnp.float32)
    mydev = row * ncol + col

    def fold(a):
        out = a[:, :128]
        for j in range(128, a.shape[1], 128):
            out += a[:, j : j + 128]
        return out

    def split(a):
        near = a.astype(jnp.bfloat16)
        return near, (a - near.astype(jnp.float32)).astype(jnp.bfloat16)

    def plus(a, b):
        return b if a is None else a + b

    def tile(n, chip):
        nonlocal moment, spread, weight
        block = cbuf[pl.ds(chip * 2, 2)].reshape(wide, width)
        hcol = hc[pl.ds(chip * 2, 2)].reshape(wide, rank)
        col_sq = jnp.sum(squares(block).T, axis=0, keepdims=True)
        weight += jnp.sum(hcol.astype(jnp.float32), axis=0, keepdims=True)
        below = None
        for b in range(bands):
            mat = rbuf[b * group : (b + 1) * group].reshape(tall, width)
            hrow = hr[b * group : (b + 1) * group].reshape(tall, rank)
            if row_sq[b] is None:
                row_sq[b] = jnp.sum(squares(mat), axis=1, keepdims=True)
            inner = lax.dot_general(hrow, hcol, (((1,), (1,)), ((), ())), preferred_element_type=jnp.float32)
            spread += jnp.sum(fold(inner * inner), axis=0, keepdims=True)
            gram = lax.dot_general(mat, block, (((1,), (1,)), ((), ())), preferred_element_type=jnp.float32)
            k = jnp.exp((2.0 * gram - row_sq[b] - col_sq) * (0.5 / width))
            ksend[b * group : (b + 1) * group, chip] = k.reshape(group, rows, wide)
            left = jnp.concatenate([*split(k), *split(inner)], axis=0)
            prod = jnp.dot(left, hcol, preferred_element_type=jnp.float32)
            drawn = prod[:tall] + prod[tall : 2 * tall]
            moment += jnp.sum(drawn, axis=0, keepdims=True)
            forces[b] = plus(forces[b], prod[2 * tall : 3 * tall] + prod[3 * tall :] - drawn)
            row_acc[b] = plus(row_acc[b], fold(k))
            below = plus(below, jnp.sum(k, axis=0, keepdims=True))
        csum[mydev, n] = below
        tots.append(fold(below))
        if n < nz - 1:
            rows_out(chip)

    def rows_out(chip):
        for p in range(nr - 1, 0, -1):
            send(ksend.at[row_peer(p, 1), chip], krecv.at[rid, chip], "kern", ("kern", p), in_plane(p))

    for k in range(1, side):
        arrive(rbuf.at[y * side + at_x(k, -1)], "rpts", ("rx", k))
        arrive(hr.at[y * side + at_x(k, -1)], "rfac", ("hx", k))
    for ky in range(1, side):
        for kx in range(1, side):
            other = at_y(ky, -1) * side + at_x(kx, -1)
            for c in range(cuts):
                arrive(rbuf.at[other, part(c)], "rpts", ("rd", ky, kx, c))
            arrive(hr.at[other], "rfac", ("hd", ky, kx))
    for n in range(nz):
        if n == nz - 1 and nz > 2:
            for c in order:
                pass_along(n, c)
        chip = line_order(z, nz, n, jnp.minimum)
        cross_wait(chip)
        tile(n, chip)

    tot = sum(tots[1:], tots[0])
    both = [jnp.broadcast_to(jnp.sum(one, axis=1, keepdims=True), (1, 128)) for one in (tot, spread)]
    first_half = lax.broadcasted_iota(jnp.int32, (1, 128), 1) < 64
    tsum[mydev] = jnp.concatenate([moment, jnp.where(first_half, both[0], both[1])], axis=1)
    rsum[rid, 1, :, :rank] = weight
    for b in range(bands):
        rsum[rid, 0, :, b * tall : (b + 1) * tall] = jnp.sum(row_acc[b].T, axis=0, keepdims=True)

    def each(count, action):
        def body(k, carry):
            action(k)
            return carry

        lax.fori_loop(1, count, body, 0, unroll=count <= 32)

    def total_to(k):
        there = ((row + k // ncol) % nrow, (col + k % ncol) % ncol)
        send(tsum.at[mydev], tsum.at[mydev], "tsum", ("tsum",), there)

    each(nrow * ncol, total_to)
    for n in range(1, nr):
        send(rsum.at[rid], rsum.at[rid], "rsum", ("rsum",), in_plane(n))
    def to_row_group(src, dst, kind):
        for n in range(nr - 1, 0, -1):
            send(src.at[row_peer(n, 1)], dst.at[rid], kind, (kind, n), in_plane(n))

    for b in range(bands):
        psend[b * group : (b + 1) * group] = forces[b].reshape(group, rows, rank)
    to_row_group(psend, precv, "pull")
    rows_out(line_order(z, nz, nz - 1, jnp.minimum))

    def sums_to(k):
        there = ((row + k // ncol) % nrow, (col + k % ncol) % ncol)
        send(csum.at[mydev], csum.at[mydev], "csum", ("csum",), there)

    each(nrow * ncol, sums_to)

    def gram_of(block):
        return lax.dot_general(block, block, (((0,), (0,)), ((), ())), preferred_element_type=jnp.float32)

    arrive(rsum.at[pl.ds(0, nr - 1)], "rsum", ("rsum",))
    arrive(tsum.at[pl.ds(0, nrow * ncol - 1)], "tsum", ("tsum",))
    sums = jnp.sum(tsum[...], axis=0)
    moment = sums[:, :rank] / total
    grand = sums[:, rank : rank + 1] / (total * total)
    scale = 0.5 / jnp.sqrt(sums[:, rank + 64 : rank + 65] + 1e-06)
    weight = jnp.sum(rsum[:, 1], axis=0)[:, :rank]
    row_mean = jnp.sum(rsum[:, 0], axis=0) / total
    for b in range(bands):
        means[b * tall : (b + 1) * tall] = jnp.broadcast_to(row_mean[:, b * tall : (b + 1) * tall], (128, tall)).T

    own_mean = means[pl.ds(pl.multiple_of(rid * rows, rows), rows)]
    mean = jnp.concatenate([own_mean] * (rank // 128), axis=1)
    centre = 1.0 - 2.0 * mean + grand
    rounding = centre.astype(jnp.bfloat16).astype(jnp.float32) - centre
    force = mean * weight + (moment - grand * weight) - rounding * hb.astype(jnp.float32) + psend[rid]
    for n in range(1, nr):
        arrive(precv.at[row_peer(n, -1)], "pull", ("pull", n))
        force += precv[row_peer(n, -1)]
    h = jnp.maximum(h - scale * force, 0.0)

    def held(n, p):
        return later.at[(at_z(n, -1) * nr + row_peer(p, -1)) * 2 + core]

    def along_z():
        for n in range(nz - 1, 0, -1):
            send(held(0, 0), held(0, 0), "later", ("z", n), device(at_z(n, 1), y, x))

    def over_plane(n):
        block = held(n, 0)
        if n:
            arrive(block, "later", ("z", n))
        for p in range(nr - 1, 0, -1):
            if n != 1:
                send(block, block, "later", ("plane", n, p), in_plane(p))
        send(block, block, "later", ("partner", n), partner)

    def to_partner(n):
        for p in range(1, nr):
            arrive(held(n, p), "later", ("plane", n, p))
            if n == 0 and nz > 1:
                send(held(0, p), held(0, p), "later", ("plane", 1, p), device(at_z(1, 1), y, x))
            send(held(n, p), held(n, p), "later", ("partner", n), partner)

    later[(z * nr + rid) * 2 + core] = h.astype(jnp.bfloat16)
    along_z()
    over_plane(0)
    krecv[rid] = ksend[rid]
    for n in range(1, nr):
        arrive(krecv.at[row_peer(n, -1)], "kern", ("kern", n))
    arrive(csum.at[pl.ds(0, nrow * ncol - 1)], "csum", ("csum",))
    across = jnp.concatenate([own_mean] * (wide // 128), axis=1) - grand
    for q in range(nr):
        col_sum = {}
        for source in range(nz):
            for n in range(nz):
                c = line_order(source, nz, n, min)
                for one in range(2):
                    value = csum[(source * 2 + one) * ncol + q, n]
                    col_sum[c] = value + col_sum[c] if c in col_sum else value
        for c in range(nz):
            aff[q, c] = (krecv[q, c] - across - col_sum[c] / total).astype(jnp.bfloat16)
    ah = jnp.zeros((rows, rank), jnp.float32)
    hh = jnp.zeros((rank, rank), jnp.float32)

    def use(n):
        nonlocal ah, hh
        arrive(later.at[pl.ds(0, nr)], "later", ("partner", n))
        c = at_z(n, -1)
        block = later[pl.ds(c * nr * 2, nr * 2)].reshape(nr * wide, rank)
        slab = jnp.concatenate([aff[r, c] for r in range(nr)], axis=1)
        ah += jnp.dot(slab, block, preferred_element_type=jnp.float32)
        hh += gram_of(block)

    if nz > 1:
        over_plane(1)
    to_partner(0)
    for n in range(2, nz):
        over_plane(n)
    use(0)
    for n in range(1, nz):
        to_partner(n)
        if n > 1:
            use(n - 1)
    if nz > 1:
        use(nz - 1)
    scale = 0.5 / jnp.sqrt(jnp.sum(hh * hh, keepdims=True) + 1e-06)
    h_near, h_rest = split(h)
    hh_near, hh_rest = split(hh)
    hhh = jnp.dot(jnp.concatenate([h_near, h_rest], axis=0), hh_near, preferred_element_type=jnp.float32)
    hhh = hhh[:rows] + hhh[rows:] + jnp.dot(h_near, hh_rest, preferred_element_type=jnp.float32)
    out_ref[...] = jnp.maximum(h - scale * (hhh - ah), 0.0) / unit

    def sent(ref, kind):
        remote(ref, ref, kind, ("tsum",), partner).wait_send()

    sent(rbuf.at[pl.ds(0, nr - 1)], "rpts")
    sent(hr.at[pl.ds(0, nr - 1)], "rfac")
    sent(cbuf.at[pl.ds(0, nz)], "cpart")
    sent(hc.at[pl.ds(0, nz)], "hpart")
    ends = (z + nz - 1) % nz >= nz - 2
    if nz > 1:

        @pl.when(ends)
        def _():
            sent(cbuf.at[pl.ds(0, 1)], "cline")
            sent(hc.at[pl.ds(0, 1)], "hline")

    if nz > 2:

        @pl.when(jnp.logical_not(ends))
        def _():
            sent(cbuf.at[pl.ds(0, nz + 1)], "cline")
            sent(hc.at[pl.ds(0, nz + 1)], "hline")

    sent(rsum.at[pl.ds(0, nr - 1)], "rsum")
    sent(csum.at[pl.ds(0, nrow * ncol - 1)], "csum")
    sent(tsum.at[pl.ds(0, nrow * ncol - 1)], "tsum")
    sent(psend.at[pl.ds(0, nr - 1)], "pull")
    sent(ksend.at[pl.ds(0, nr - 1)], "kern")
    sent(later.at[pl.ds(0, nrow * ncol - 1)], "later")


def solution(mesh):
    nrow, ncol = mesh.shape["row"], mesh.shape["col"]
    side, nz = layout(nrow, ncol)

    def shards(points, factor):
        rows, width = points.shape
        rank = factor.shape[1]
        wide = 2 * rows
        nr = side * side
        keys = receive_keys(nrow, ncol, rows)
        buffers = [
            ((nr, rows, width), jnp.bfloat16),
            ((2 * nz, rows, width), jnp.bfloat16),
            ((nr, rows, rank), jnp.bfloat16),
            ((2 * nz, rows, rank), jnp.bfloat16),
            ((nrow * ncol, rows, rank), jnp.bfloat16),
            ((nr, nz, rows, wide), jnp.float32),
            ((nr, nz, rows, wide), jnp.float32),
            ((nr, rows, rank), jnp.float32),
            ((nr, rows, rank), jnp.float32),
            ((nr, nz, rows, wide), jnp.bfloat16),
            ((nr * rows, 128), jnp.float32),
            ((nr, 2, 1, max(nr * rows, rank)), jnp.float32),
            ((nrow * ncol, nz, 1, wide), jnp.float32),
            ((nrow * ncol, 1, rank + 128), jnp.float32),
        ]
        held = sum(math.prod(shape) * jnp.dtype(kind).itemsize for shape, kind in buffers)
        return pl.pallas_call(
            functools.partial(kernel, nrow, ncol, keys),
            out_shape=jax.ShapeDtypeStruct((rows, rank), jnp.float32),
            in_specs=[pl.BlockSpec(memory_space=pltpu.VMEM)] * 2,
            out_specs=pl.BlockSpec(memory_space=pltpu.VMEM),
            scratch_shapes=[pltpu.VMEM(shape, kind) for shape, kind in buffers]
            + [pltpu.SemaphoreType.DMA((len(SENDS),)), pltpu.SemaphoreType.DMA((len(keys),))],
            compiler_params=pltpu.CompilerParams(
                collective_id=0, has_side_effects=True, vmem_limit_bytes=min(67043328, held + (16 << 20))
            ),
        )(points, factor)

    spec = P(("row", "col"), None)
    return jax.shard_map(shards, mesh=mesh, in_specs=(spec, spec), out_specs=spec, check_vma=False)
```

```python
import functools
import math

import jax
import jax.numpy as jnp
from jax import lax
from jax.experimental import pallas as pl
from jax.experimental.pallas import tpu as pltpu
from jax.sharding import PartitionSpec as P

MESH = pl.DeviceIdType.MESH

SENDS = ("word", "rpts", "cline", "cpart", "rfac", "hline", "hpart", "later", "rsum", "csum", "tsum", "pull", "kern")


def layout(nrow, ncol):
    return math.isqrt(ncol), nrow // 2


def cuts_of(rows):
    return 4 if rows % 64 == 0 else 1


def receive_keys(nrow, ncol, rows):
    side, nz = layout(nrow, ncol)
    cuts, plane = cuts_of(rows), side * side
    keys = [(name, k) for name in ("rx", "hx", "hy", "word") for k in range(1, side)]
    keys += [("ry", k, c) for k in range(1, side) for c in range(cuts)]
    keys += [("rd", j, k, c) for j in range(1, side) for k in range(1, side) for c in range(cuts)]
    keys += [("hd", j, k) for j in range(1, side) for k in range(1, side)]
    keys += [("line", k) for k in range(nz * (cuts + 1))]
    keys += [("cross", k) for k in range(nz * 2)]
    keys += [("rsum",), ("csum",), ("tsum",)]
    keys += [(name, k) for name in ("kern", "pull") for k in range(1, plane)]
    keys += [("z", k) for k in range(1, nz)]
    keys += [("plane", k, p) for k in range(nz) for p in range(1, plane)]
    keys += [("partner", k) for k in range(nz)]
    return {key: i for i, key in enumerate(keys)}


def line_order(z, nz, n, least):
    if not n:
        return z
    up = 2 * z // nz
    sign, near = 1 - 2 * up, z + up * (nz - 1 - 2 * z)
    paired = least(near // ((n + 1) // 2), 1)
    return z + sign * (paired * (-((n + 1) // 2) if n % 2 else n // 2) + (1 - paired) * (n - near))


def shift(i, k, n, sign):
    if n & (n - 1) or n == 2:
        return (i + sign * k + n) % n
    out, bit = i, 1
    while bit < n:
        if k & bit:
            out = out + bit - 2 * bit * ((i // bit) % 2)
        bit *= 2
    return out


def kernel(nrow, ncol, keys, pts_ref, fac_ref, out_ref, words, rbuf, cbuf, hr, hc, later, ksend, krecv, psend, precv, aff, means, rsum, csum, tsum, ssem, rsem):
    side, nz = layout(nrow, ncol)
    rows, width = pts_ref.shape
    rank = fac_ref.shape[1]
    wide = 2 * rows
    nr = side * side
    total = rows * nrow * ncol
    unit = 2.0 / math.sqrt(total * rank)
    cuts = cuts_of(rows)
    piece = rows // cuts
    row, col = lax.axis_index("row"), lax.axis_index("col")
    z, core = row // 2, row % 2
    y, x = col // side, col % side
    rid = y * side + x
    partner = (z * 2 + 1 - core, col)

    def device(zz, yy, xx):
        return (zz * 2 + core, yy * side + xx)

    def at_z(k, sign):
        return shift(z, k, nz, sign)

    def at_y(k, sign):
        return (y + sign * k + side) % side

    def at_x(k, sign):
        return (x + sign * k + side) % side

    def remote(src, dst, kind, key, where):
        return pltpu.make_async_remote_copy(
            src_ref=src,
            dst_ref=dst,
            send_sem=ssem.at[SENDS.index(kind)],
            recv_sem=rsem.at[keys[key]],
            device_id=where,
            device_id_type=MESH,
        )

    def send(src, dst, kind, key, where):
        remote(src, dst, kind, key, where).start()

    def arrive(block, kind, key):
        remote(block, block, kind, key, partner).wait_recv()

    plane = [(ky, kx) for ky in range(side) for kx in range(side)]

    def row_peer(n, sign):
        ky, kx = plane[n]
        return at_y(ky, sign) * side + at_x(kx, sign)

    def in_plane(n):
        ky, kx = plane[n]
        return device(z, at_y(ky, 1), at_x(kx, 1))

    barrier = pltpu.get_barrier_semaphore()
    peers = [device(z, y, at_x(k, 1)) for k in range(1, side)]
    peers += [device(z, at_y(k, 1), x) for k in range(1, side)]
    peers.append(partner)
    for peer in peers:
        pl.semaphore_signal(barrier, inc=1, device_id=peer, device_id_type=MESH)
    not_low, not_high = z > 0, z < nz - 1

    @pl.when(not_low)
    def _():
        pl.semaphore_signal(barrier, inc=1, device_id=device(z - 1, y, x), device_id_type=MESH)

    @pl.when(not_high)
    def _():
        pl.semaphore_signal(barrier, inc=1, device_id=device(z + 1, y, x), device_id_type=MESH)

    h = fac_ref[...] * unit
    hb = h.astype(jnp.bfloat16)
    hr[rid] = hb
    hc[z * 2 + core] = hb
    rbuf[rid] = pts_ref[...]
    cbuf[z * 2 + core] = pts_ref[...]
    pl.semaphore_wait(barrier, len(peers) + jnp.minimum(z, 1) + jnp.minimum(nz - 1 - z, 1))

    def part(c):
        return pl.ds(c * piece, piece)

    def line_copy(src, c, where=None, local=None):
        block = hc.at[src * 2 + core] if c == cuts else cbuf.at[src * 2 + core, part(c)]
        return pltpu.make_async_remote_copy(
            src_ref=block if local is None else local,
            dst_ref=block,
            send_sem=ssem.at[SENDS.index("hline" if c == cuts else "cline")],
            recv_sem=rsem.at[keys["line", 0] + src * (cuts + 1) + c],
            device_id=partner if where is None else device(where, y, x),
            device_id_type=MESH,
        )

    def cross_copy(src, c, local=None):
        slot = src * 2 + core
        block = hc.at[slot] if c == cuts else cbuf.at[slot] if c is None else cbuf.at[slot, part(c)]
        return pltpu.make_async_remote_copy(
            src_ref=block if local is None else local,
            dst_ref=block,
            send_sem=ssem.at[SENDS.index("hpart" if c == cuts else "cpart")],
            recv_sem=rsem.at[keys["cross", 0] + src * 2 + (1 if c == cuts else 0)],
            device_id=partner,
            device_id_type=MESH,
        )

    def cross_wait(src):
        for block, k in ((cbuf.at[src * 2 + 1 - core], 0), (hc.at[src * 2 + 1 - core], 1)):
            pltpu.make_async_remote_copy(
                src_ref=block,
                dst_ref=block,
                send_sem=ssem.at[0],
                recv_sem=rsem.at[keys["cross", 0] + src * 2 + k],
                device_id=partner,
                device_id_type=MESH,
            ).wait_recv()

    def own_piece(c):
        local = None if c == cuts else pts_ref.at[part(c)]

        @pl.when(not_low)
        def _():
            line_copy(z, c, z - 1, local).start()

        @pl.when(not_high)
        def _():
            line_copy(z, c, z + 1, local).start()

    short = pl.ds(0, 8), pl.ds(0, 128)
    for k in range(1, side):
        send(fac_ref.at[short], words.at[y], "word", ("word", k), device(z, at_y(k, 1), x))
    order = [cuts, *range(cuts)]
    for c in order[:-1]:
        own_piece(c)
    for k in range(1, side):
        send(hr.at[rid], hr.at[rid], "rfac", ("hy", k), device(z, at_y(k, 1), x))
        send(hr.at[rid], hr.at[rid], "rfac", ("hx", k), device(z, y, at_x(k, 1)))
    for c in range(cuts):
        for k in range(1, side):
            send(pts_ref.at[part(c)], rbuf.at[rid, part(c)], "rpts", ("ry", k, c), device(z, at_y(k, 1), x))
    for k in range(1, side):
        send(pts_ref, rbuf.at[rid], "rpts", ("rx", k), device(z, y, at_x(k, 1)))
    cross_copy(z, None, pts_ref).start()
    cross_copy(z, cuts).start()

    def pass_along(d, c):
        @pl.when(z + d < nz)
        def _():
            line_copy(z + d, c).wait_recv()

            @pl.when(not_low)
            def _():
                line_copy(z + d, c, z - 1).start()

            cross_copy(z + d, c).start()

        @pl.when(z >= d)
        def _():
            line_copy(z - d, c).wait_recv()

            @pl.when(not_high)
            def _():
                line_copy(z - d, c, z + 1).start()

            cross_copy(z - d, c).start()

    def pass_over(c):
        for k in range(1, side):
            other = at_y(k, -1) * side + x
            block = hr.at[other] if c == cuts else rbuf.at[other, part(c)]
            kind, key = ("rfac", ("hy", k)) if c == cuts else ("rpts", ("ry", k, c))
            arrive(block, kind, key)
            for kx in range(1, side):
                key = ("hd", k, kx) if c == cuts else ("rd", k, kx, c)
                send(block, block, kind, key, device(z, y, at_x(kx, 1)))

    for c in order:
        if c == cuts:
            for k in range(1, side):
                arrive(words.at[at_y(k, -1)], "word", ("word", k))
            own_piece(order[-1])
        pass_over(c)
        if nz > 1:
            pass_along(1, c)
    for d in range(2, nz - 1):
        for c in order:
            pass_along(d, c)

    def squares(block):
        acc = None
        for k in range(0, width, 128):
            one = block[:, k : k + 128].astype(jnp.float32)
            acc = one * one if acc is None else acc + one * one
        return acc

    tall = min(nr * rows, 256)
    bands, group = nr * rows // tall, tall // rows
    row_sq, row_acc, forces, tots = [None] * bands, [None] * bands, [None] * bands, []
    moment = jnp.zeros((1, rank), jnp.float32)
    spread = jnp.zeros((1, 128), jnp.float32)
    weight = jnp.zeros((1, rank), jnp.float32)
    mydev = row * ncol + col

    def fold(a):
        out = a[:, :128]
        for j in range(128, a.shape[1], 128):
            out += a[:, j : j + 128]
        return out

    def split(a):
        near = a.astype(jnp.bfloat16)
        return near, (a - near.astype(jnp.float32)).astype(jnp.bfloat16)

    def plus(a, b):
        return b if a is None else a + b

    def tile(n, chip):
        nonlocal moment, spread, weight
        block = cbuf[pl.ds(chip * 2, 2)].reshape(wide, width)
        hcol = hc[pl.ds(chip * 2, 2)].reshape(wide, rank)
        col_sq = jnp.sum(squares(block).T, axis=0, keepdims=True)
        weight += jnp.sum(hcol.astype(jnp.float32), axis=0, keepdims=True)
        below = None
        for b in range(bands):
            mat = rbuf[b * group : (b + 1) * group].reshape(tall, width)
            hrow = hr[b * group : (b + 1) * group].reshape(tall, rank)
            if row_sq[b] is None:
                row_sq[b] = jnp.sum(squares(mat), axis=1, keepdims=True)
            inner = lax.dot_general(hrow, hcol, (((1,), (1,)), ((), ())), preferred_element_type=jnp.float32)
            spread += jnp.sum(fold(inner * inner), axis=0, keepdims=True)
            gram = lax.dot_general(mat, block, (((1,), (1,)), ((), ())), preferred_element_type=jnp.float32)
            k = jnp.exp((2.0 * gram - row_sq[b] - col_sq) * (0.5 / width))
            ksend[b * group : (b + 1) * group, chip] = k.reshape(group, rows, wide)
            left = jnp.concatenate([*split(k), *split(inner)], axis=0)
            prod = jnp.dot(left, hcol, preferred_element_type=jnp.float32)
            drawn = prod[:tall] + prod[tall : 2 * tall]
            moment += jnp.sum(drawn, axis=0, keepdims=True)
            forces[b] = plus(forces[b], prod[2 * tall : 3 * tall] + prod[3 * tall :] - drawn)
            row_acc[b] = plus(row_acc[b], fold(k))
            below = plus(below, jnp.sum(k, axis=0, keepdims=True))
        csum[mydev, n] = below
        tots.append(fold(below))
        if n < nz - 1:
            rows_out(chip)

    def rows_out(chip):
        for p in range(nr - 1, 0, -1):
            send(ksend.at[row_peer(p, 1), chip], krecv.at[rid, chip], "kern", ("kern", p), in_plane(p))

    for k in range(1, side):
        arrive(rbuf.at[y * side + at_x(k, -1)], "rpts", ("rx", k))
        arrive(hr.at[y * side + at_x(k, -1)], "rfac", ("hx", k))
    for ky in range(1, side):
        for kx in range(1, side):
            other = at_y(ky, -1) * side + at_x(kx, -1)
            for c in range(cuts):
                arrive(rbuf.at[other, part(c)], "rpts", ("rd", ky, kx, c))
            arrive(hr.at[other], "rfac", ("hd", ky, kx))
    for n in range(nz):
        if n == nz - 1 and nz > 2:
            for c in order:
                pass_along(n, c)
        chip = line_order(z, nz, n, jnp.minimum)
        cross_wait(chip)
        tile(n, chip)

    tot = sum(tots[1:], tots[0])
    both = [jnp.broadcast_to(jnp.sum(one, axis=1, keepdims=True), (1, 128)) for one in (tot, spread)]
    first_half = lax.broadcasted_iota(jnp.int32, (1, 128), 1) < 64
    tsum[mydev] = jnp.concatenate([moment, jnp.where(first_half, both[0], both[1])], axis=1)
    rsum[rid, 1, :, :rank] = weight
    for b in range(bands):
        rsum[rid, 0, :, b * tall : (b + 1) * tall] = jnp.sum(row_acc[b].T, axis=0, keepdims=True)

    def each(count, action):
        def body(k, carry):
            action(k)
            return carry

        lax.fori_loop(1, count, body, 0, unroll=count <= 32)

    def total_to(k):
        there = ((row + k // ncol) % nrow, (col + k % ncol) % ncol)
        send(tsum.at[mydev], tsum.at[mydev], "tsum", ("tsum",), there)

    each(nrow * ncol, total_to)
    for n in range(1, nr):
        send(rsum.at[rid], rsum.at[rid], "rsum", ("rsum",), in_plane(n))
    def to_row_group(src, dst, kind):
        for n in range(nr - 1, 0, -1):
            send(src.at[row_peer(n, 1)], dst.at[rid], kind, (kind, n), in_plane(n))

    for b in range(bands):
        psend[b * group : (b + 1) * group] = forces[b].reshape(group, rows, rank)
    to_row_group(psend, precv, "pull")
    rows_out(line_order(z, nz, nz - 1, jnp.minimum))

    def sums_to(k):
        there = ((row + k // ncol) % nrow, (col + k % ncol) % ncol)
        send(csum.at[mydev], csum.at[mydev], "csum", ("csum",), there)

    each(nrow * ncol, sums_to)

    def gram_of(block):
        return lax.dot_general(block, block, (((0,), (0,)), ((), ())), preferred_element_type=jnp.float32)

    arrive(rsum.at[pl.ds(0, nr - 1)], "rsum", ("rsum",))
    arrive(tsum.at[pl.ds(0, nrow * ncol - 1)], "tsum", ("tsum",))
    sums = jnp.sum(tsum[...], axis=0)
    moment = sums[:, :rank] / total
    grand = sums[:, rank : rank + 1] / (total * total)
    scale = 0.5 / jnp.sqrt(sums[:, rank + 64 : rank + 65] + 1e-06)
    weight = jnp.sum(rsum[:, 1], axis=0)[:, :rank]
    row_mean = jnp.sum(rsum[:, 0], axis=0) / total
    for b in range(bands):
        means[b * tall : (b + 1) * tall] = jnp.broadcast_to(row_mean[:, b * tall : (b + 1) * tall], (128, tall)).T

    own_mean = means[pl.ds(pl.multiple_of(rid * rows, rows), rows)]
    mean = jnp.concatenate([own_mean] * (rank // 128), axis=1)
    centre = 1.0 - 2.0 * mean + grand
    rounding = centre.astype(jnp.bfloat16).astype(jnp.float32) - centre
    force = mean * weight + (moment - grand * weight) - rounding * hb.astype(jnp.float32) + psend[rid]
    for n in range(1, nr):
        arrive(precv.at[row_peer(n, -1)], "pull", ("pull", n))
        force += precv[row_peer(n, -1)]
    h = jnp.maximum(h - scale * force, 0.0)

    def held(n, p):
        return later.at[(at_z(n, -1) * nr + row_peer(p, -1)) * 2 + core]

    def along_z():
        for n in range(nz - 1, 0, -1):
            send(held(0, 0), held(0, 0), "later", ("z", n), device(at_z(n, 1), y, x))

    def over_plane(n):
        block = held(n, 0)
        if n:
            arrive(block, "later", ("z", n))
        for p in range(nr - 1, 0, -1):
            if n != 1:
                send(block, block, "later", ("plane", n, p), in_plane(p))
        send(block, block, "later", ("partner", n), partner)

    def to_partner(n):
        for p in range(1, nr):
            arrive(held(n, p), "later", ("plane", n, p))
            if n == 0 and nz > 1:
                send(held(0, p), held(0, p), "later", ("plane", 1, p), device(at_z(1, 1), y, x))
            send(held(n, p), held(n, p), "later", ("partner", n), partner)

    later[(z * nr + rid) * 2 + core] = h.astype(jnp.bfloat16)
    along_z()
    over_plane(0)
    krecv[rid] = ksend[rid]
    for n in range(1, nr):
        arrive(krecv.at[row_peer(n, -1)], "kern", ("kern", n))
    arrive(csum.at[pl.ds(0, nrow * ncol - 1)], "csum", ("csum",))
    across = jnp.concatenate([own_mean] * (wide // 128), axis=1) - grand
    for q in range(nr):
        col_sum = {}
        for source in range(nz):
            for n in range(nz):
                c = line_order(source, nz, n, min)
                for one in range(2):
                    value = csum[(source * 2 + one) * ncol + q, n]
                    col_sum[c] = value + col_sum[c] if c in col_sum else value
        for c in range(nz):
            aff[q, c] = (krecv[q, c] - across - col_sum[c] / total).astype(jnp.bfloat16)
    ah = jnp.zeros((rows, rank), jnp.float32)
    hh = jnp.zeros((rank, rank), jnp.float32)

    def use(n):
        nonlocal ah, hh
        arrive(later.at[pl.ds(0, nr)], "later", ("partner", n))
        c = at_z(n, -1)
        block = later[pl.ds(c * nr * 2, nr * 2)].reshape(nr * wide, rank)
        slab = jnp.concatenate([aff[r, c] for r in range(nr)], axis=1)
        ah += jnp.dot(slab, block, preferred_element_type=jnp.float32)
        hh += gram_of(block)

    if nz > 1:
        over_plane(1)
    to_partner(0)
    for n in range(2, nz):
        over_plane(n)
    use(0)
    for n in range(1, nz):
        to_partner(n)
        if n > 1:
            use(n - 1)
    if nz > 1:
        use(nz - 1)
    scale = 0.5 / jnp.sqrt(jnp.sum(hh * hh, keepdims=True) + 1e-06)
    h_near, h_rest = split(h)
    hh_near, hh_rest = split(hh)
    hhh = jnp.dot(jnp.concatenate([h_near, h_rest], axis=0), hh_near, preferred_element_type=jnp.float32)
    hhh = hhh[:rows] + hhh[rows:] + jnp.dot(h_near, hh_rest, preferred_element_type=jnp.float32)
    out_ref[...] = jnp.maximum(h - scale * (hhh - ah), 0.0) / unit

    def sent(ref, kind):
        remote(ref, ref, kind, ("tsum",), partner).wait_send()

    sent(words.at[pl.ds(0, side - 1)], "word")
    sent(rbuf.at[pl.ds(0, nr - 1)], "rpts")
    sent(hr.at[pl.ds(0, nr - 1)], "rfac")
    sent(cbuf.at[pl.ds(0, nz)], "cpart")
    sent(hc.at[pl.ds(0, nz)], "hpart")
    ends = (z + nz - 1) % nz >= nz - 2
    if nz > 1:

        @pl.when(ends)
        def _():
            sent(cbuf.at[pl.ds(0, 1)], "cline")
            sent(hc.at[pl.ds(0, 1)], "hline")

    if nz > 2:

        @pl.when(jnp.logical_not(ends))
        def _():
            sent(cbuf.at[pl.ds(0, nz + 1)], "cline")
            sent(hc.at[pl.ds(0, nz + 1)], "hline")

    sent(rsum.at[pl.ds(0, nr - 1)], "rsum")
    sent(csum.at[pl.ds(0, nrow * ncol - 1)], "csum")
    sent(tsum.at[pl.ds(0, nrow * ncol - 1)], "tsum")
    sent(psend.at[pl.ds(0, nr - 1)], "pull")
    sent(ksend.at[pl.ds(0, nr - 1)], "kern")
    sent(later.at[pl.ds(0, nrow * ncol - 1)], "later")


def solution(mesh):
    nrow, ncol = mesh.shape["row"], mesh.shape["col"]
    side, nz = layout(nrow, ncol)

    def shards(points, factor):
        rows, width = points.shape
        rank = factor.shape[1]
        wide = 2 * rows
        nr = side * side
        keys = receive_keys(nrow, ncol, rows)
        buffers = [
            ((side, 8, 128), jnp.float32),
            ((nr, rows, width), jnp.bfloat16),
            ((2 * nz, rows, width), jnp.bfloat16),
            ((nr, rows, rank), jnp.bfloat16),
            ((2 * nz, rows, rank), jnp.bfloat16),
            ((nrow * ncol, rows, rank), jnp.bfloat16),
            ((nr, nz, rows, wide), jnp.float32),
            ((nr, nz, rows, wide), jnp.float32),
            ((nr, rows, rank), jnp.float32),
            ((nr, rows, rank), jnp.float32),
            ((nr, nz, rows, wide), jnp.bfloat16),
            ((nr * rows, 128), jnp.float32),
            ((nr, 2, 1, max(nr * rows, rank)), jnp.float32),
            ((nrow * ncol, nz, 1, wide), jnp.float32),
            ((nrow * ncol, 1, rank + 128), jnp.float32),
        ]
        held = sum(math.prod(shape) * jnp.dtype(kind).itemsize for shape, kind in buffers)
        return pl.pallas_call(
            functools.partial(kernel, nrow, ncol, keys),
            out_shape=jax.ShapeDtypeStruct((rows, rank), jnp.float32),
            in_specs=[pl.BlockSpec(memory_space=pltpu.VMEM)] * 2,
            out_specs=pl.BlockSpec(memory_space=pltpu.VMEM),
            scratch_shapes=[pltpu.VMEM(shape, kind) for shape, kind in buffers]
            + [pltpu.SemaphoreType.DMA((len(SENDS),)), pltpu.SemaphoreType.DMA((len(keys),))],
            compiler_params=pltpu.CompilerParams(
                collective_id=0, has_side_effects=True, vmem_limit_bytes=min(67043328, held + (16 << 20))
            ),
        )(points, factor)

    spec = P(("row", "col"), None)
    return jax.shard_map(shards, mesh=mesh, in_specs=(spec, spec), out_specs=spec, check_vma=False)
```

```python
import functools
import math

import jax
import jax.numpy as jnp
from jax import lax
from jax.experimental import pallas as pl
from jax.experimental.pallas import tpu as pltpu
from jax.sharding import PartitionSpec as P

MESH = pl.DeviceIdType.MESH

SENDS = ("word", "rpts", "cline", "cpart", "rfac", "hline", "hpart", "later", "rsum", "csum", "tsum", "pull", "kern")


def layout(nrow, ncol):
    return math.isqrt(ncol), nrow // 2


def cuts_of(rows):
    return 4 if rows % 64 == 0 else 1


def receive_keys(nrow, ncol, rows):
    side, nz = layout(nrow, ncol)
    cuts, plane = cuts_of(rows), side * side
    keys = [(name, k) for name in ("rx", "hx", "hy", "word") for k in range(1, side)]
    keys += [("ry", k, c) for k in range(1, side) for c in range(cuts)]
    keys += [("rd", j, k, c) for j in range(1, side) for k in range(1, side) for c in range(cuts)]
    keys += [("hd", j, k) for j in range(1, side) for k in range(1, side)]
    keys += [("line", k) for k in range(nz * (cuts + 1))]
    keys += [("cross", k) for k in range(nz * 2)]
    keys += [("rsum",), ("csum",), ("tsum",)]
    keys += [(name, k) for name in ("kern", "pull") for k in range(1, plane)]
    keys += [("z", k) for k in range(1, nz)]
    keys += [("plane", k, p) for k in range(nz) for p in range(1, plane)]
    keys += [("partner", k) for k in range(nz)]
    return {key: i for i, key in enumerate(keys)}


def line_order(z, nz, n, least):
    if not n:
        return z
    up = 2 * z // nz
    sign, near = 1 - 2 * up, z + up * (nz - 1 - 2 * z)
    paired = least(near // ((n + 1) // 2), 1)
    return z + sign * (paired * (-((n + 1) // 2) if n % 2 else n // 2) + (1 - paired) * (n - near))


def shift(i, k, n, sign):
    if n & (n - 1) or n == 2:
        return (i + sign * k + n) % n
    out, bit = i, 1
    while bit < n:
        if k & bit:
            out = out + bit - 2 * bit * ((i // bit) % 2)
        bit *= 2
    return out


def kernel(nrow, ncol, keys, pts_ref, fac_ref, out_ref, words, rbuf, cbuf, hr, hc, later, ksend, krecv, psend, precv, aff, means, rsum, csum, tsum, ssem, rsem):
    side, nz = layout(nrow, ncol)
    rows, width = pts_ref.shape
    rank = fac_ref.shape[1]
    wide = 2 * rows
    nr = side * side
    total = rows * nrow * ncol
    unit = 2.0 / math.sqrt(total * rank)
    cuts = cuts_of(rows)
    piece = rows // cuts
    row, col = lax.axis_index("row"), lax.axis_index("col")
    z, core = row // 2, row % 2
    y, x = col // side, col % side
    rid = y * side + x
    partner = (z * 2 + 1 - core, col)

    def device(zz, yy, xx):
        return (zz * 2 + core, yy * side + xx)

    def at_z(k, sign):
        return shift(z, k, nz, sign)

    def at_y(k, sign):
        return (y + sign * k + side) % side

    def at_x(k, sign):
        return (x + sign * k + side) % side

    def remote(src, dst, kind, key, where):
        return pltpu.make_async_remote_copy(
            src_ref=src,
            dst_ref=dst,
            send_sem=ssem.at[SENDS.index(kind)],
            recv_sem=rsem.at[keys[key]],
            device_id=where,
            device_id_type=MESH,
        )

    def send(src, dst, kind, key, where):
        remote(src, dst, kind, key, where).start()

    def arrive(block, kind, key):
        remote(block, block, kind, key, partner).wait_recv()

    plane = [(ky, kx) for ky in range(side) for kx in range(side)]

    def row_peer(n, sign):
        ky, kx = plane[n]
        return at_y(ky, sign) * side + at_x(kx, sign)

    def in_plane(n):
        ky, kx = plane[n]
        return device(z, at_y(ky, 1), at_x(kx, 1))

    barrier = pltpu.get_barrier_semaphore()
    peers = [device(z, y, at_x(k, 1)) for k in range(1, side)]
    peers += [device(z, at_y(k, 1), x) for k in range(1, side)]
    peers.append(partner)
    for peer in peers:
        pl.semaphore_signal(barrier, inc=1, device_id=peer, device_id_type=MESH)
    not_low, not_high = z > 0, z < nz - 1

    @pl.when(not_low)
    def _():
        pl.semaphore_signal(barrier, inc=1, device_id=device(z - 1, y, x), device_id_type=MESH)

    @pl.when(not_high)
    def _():
        pl.semaphore_signal(barrier, inc=1, device_id=device(z + 1, y, x), device_id_type=MESH)

    h = fac_ref[...] * unit
    hb = h.astype(jnp.bfloat16)
    hr[rid] = hb
    hc[z * 2 + core] = hb
    rbuf[rid] = pts_ref[...]
    cbuf[z * 2 + core] = pts_ref[...]
    pl.semaphore_wait(barrier, len(peers) + jnp.minimum(z, 1) + jnp.minimum(nz - 1 - z, 1))

    def part(c):
        return pl.ds(c * piece, piece)

    def line_copy(src, c, where=None, local=None):
        block = hc.at[src * 2 + core] if c == cuts else cbuf.at[src * 2 + core, part(c)]
        return pltpu.make_async_remote_copy(
            src_ref=block if local is None else local,
            dst_ref=block,
            send_sem=ssem.at[SENDS.index("hline" if c == cuts else "cline")],
            recv_sem=rsem.at[keys["line", 0] + src * (cuts + 1) + c],
            device_id=partner if where is None else device(where, y, x),
            device_id_type=MESH,
        )

    def cross_copy(src, c, local=None):
        slot = src * 2 + core
        block = hc.at[slot] if c == cuts else cbuf.at[slot] if c is None else cbuf.at[slot, part(c)]
        return pltpu.make_async_remote_copy(
            src_ref=block if local is None else local,
            dst_ref=block,
            send_sem=ssem.at[SENDS.index("hpart" if c == cuts else "cpart")],
            recv_sem=rsem.at[keys["cross", 0] + src * 2 + (1 if c == cuts else 0)],
            device_id=partner,
            device_id_type=MESH,
        )

    def cross_wait(src):
        for block, k in ((cbuf.at[src * 2 + 1 - core], 0), (hc.at[src * 2 + 1 - core], 1)):
            pltpu.make_async_remote_copy(
                src_ref=block,
                dst_ref=block,
                send_sem=ssem.at[0],
                recv_sem=rsem.at[keys["cross", 0] + src * 2 + k],
                device_id=partner,
                device_id_type=MESH,
            ).wait_recv()

    def own_piece(c):
        local = None if c == cuts else pts_ref.at[part(c)]

        @pl.when(not_low)
        def _():
            line_copy(z, c, z - 1, local).start()

        @pl.when(not_high)
        def _():
            line_copy(z, c, z + 1, local).start()

    short = pl.ds(0, 8), pl.ds(0, 128)
    for k in range(1, side):
        send(fac_ref.at[short], words.at[y], "word", ("word", k), device(z, at_y(k, 1), x))
    order = [cuts, *range(cuts)]
    for c in order[:-1]:
        own_piece(c)
    for k in range(1, side):
        send(hr.at[rid], hr.at[rid], "rfac", ("hy", k), device(z, at_y(k, 1), x))
        send(hr.at[rid], hr.at[rid], "rfac", ("hx", k), device(z, y, at_x(k, 1)))
    for c in range(cuts):
        for k in range(1, side):
            send(pts_ref.at[part(c)], rbuf.at[rid, part(c)], "rpts", ("ry", k, c), device(z, at_y(k, 1), x))
    for k in range(1, side):
        send(pts_ref, rbuf.at[rid], "rpts", ("rx", k), device(z, y, at_x(k, 1)))
    cross_copy(z, None, pts_ref).start()
    cross_copy(z, cuts).start()

    def pass_along(d, c):
        @pl.when(z + d < nz)
        def _():
            line_copy(z + d, c).wait_recv()

            @pl.when(not_low)
            def _():
                line_copy(z + d, c, z - 1).start()

            cross_copy(z + d, c).start()

        @pl.when(z >= d)
        def _():
            line_copy(z - d, c).wait_recv()

            @pl.when(not_high)
            def _():
                line_copy(z - d, c, z + 1).start()

            cross_copy(z - d, c).start()

    def pass_over(c):
        for k in range(1, side):
            other = at_y(k, -1) * side + x
            block = hr.at[other] if c == cuts else rbuf.at[other, part(c)]
            kind, key = ("rfac", ("hy", k)) if c == cuts else ("rpts", ("ry", k, c))
            arrive(block, kind, key)
            for kx in range(1, side):
                key = ("hd", k, kx) if c == cuts else ("rd", k, kx, c)
                send(block, block, kind, key, device(z, y, at_x(kx, 1)))

    for c in order:
        if c == cuts:
            for k in range(1, side):
                arrive(words.at[at_y(k, -1)], "word", ("word", k))
            own_piece(order[-1])
        pass_over(c)
        if nz > 1:
            pass_along(1, c)
    for d in range(2, nz - 1):
        for c in order:
            pass_along(d, c)

    def squares(block):
        acc = None
        for k in range(0, width, 128):
            one = block[:, k : k + 128].astype(jnp.float32)
            acc = one * one if acc is None else acc + one * one
        return acc

    tall = min(nr * rows, 256)
    bands, group = nr * rows // tall, tall // rows
    row_sq, row_acc, forces, tots = [None] * bands, [None] * bands, [None] * bands, []
    moment = jnp.zeros((1, rank), jnp.float32)
    spread = jnp.zeros((1, 128), jnp.float32)
    weight = jnp.zeros((1, rank), jnp.float32)
    mydev = row * ncol + col

    def fold(a):
        out = a[:, :128]
        for j in range(128, a.shape[1], 128):
            out += a[:, j : j + 128]
        return out

    def split(a):
        near = a.astype(jnp.bfloat16)
        return near, (a - near.astype(jnp.float32)).astype(jnp.bfloat16)

    def plus(a, b):
        return b if a is None else a + b

    def tile(n, chip):
        nonlocal moment, spread, weight
        block = cbuf[pl.ds(chip * 2, 2)].reshape(wide, width)
        hcol = hc[pl.ds(chip * 2, 2)].reshape(wide, rank)
        col_sq = jnp.sum(squares(block).T, axis=0, keepdims=True)
        weight += jnp.sum(hcol.astype(jnp.float32), axis=0, keepdims=True)
        below = None
        for b in range(bands):
            mat = rbuf[b * group : (b + 1) * group].reshape(tall, width)
            hrow = hr[b * group : (b + 1) * group].reshape(tall, rank)
            if row_sq[b] is None:
                row_sq[b] = jnp.sum(squares(mat), axis=1, keepdims=True)
            inner = lax.dot_general(hrow, hcol, (((1,), (1,)), ((), ())), preferred_element_type=jnp.float32)
            spread += jnp.sum(fold(inner * inner), axis=0, keepdims=True)
            gram = lax.dot_general(mat, block, (((1,), (1,)), ((), ())), preferred_element_type=jnp.float32)
            k = jnp.exp((2.0 * gram - row_sq[b] - col_sq) * (0.5 / width))
            ksend[b * group : (b + 1) * group, chip] = k.reshape(group, rows, wide)
            left = jnp.concatenate([*split(k), *split(inner)], axis=0)
            prod = jnp.dot(left, hcol, preferred_element_type=jnp.float32)
            drawn = prod[:tall] + prod[tall : 2 * tall]
            moment += jnp.sum(drawn, axis=0, keepdims=True)
            forces[b] = plus(forces[b], prod[2 * tall : 3 * tall] + prod[3 * tall :] - drawn)
            row_acc[b] = plus(row_acc[b], fold(k))
            below = plus(below, jnp.sum(k, axis=0, keepdims=True))
        csum[mydev, n] = below
        tots.append(fold(below))
        if n < nz - 1:
            rows_out(chip)

    def rows_out(chip):
        for p in range(nr - 1, 0, -1):
            send(ksend.at[row_peer(p, 1), chip], krecv.at[rid, chip], "kern", ("kern", p), in_plane(p))

    for k in range(1, side):
        arrive(rbuf.at[y * side + at_x(k, -1)], "rpts", ("rx", k))
        arrive(hr.at[y * side + at_x(k, -1)], "rfac", ("hx", k))
    for ky in range(1, side):
        for kx in range(1, side):
            other = at_y(ky, -1) * side + at_x(kx, -1)
            for c in range(cuts):
                arrive(rbuf.at[other, part(c)], "rpts", ("rd", ky, kx, c))
            arrive(hr.at[other], "rfac", ("hd", ky, kx))
    for n in range(nz):
        if n == nz - 1 and nz > 2:
            for c in order:
                pass_along(n, c)
        chip = line_order(z, nz, n, jnp.minimum)
        cross_wait(chip)
        tile(n, chip)

    tot = sum(tots[1:], tots[0])
    both = [jnp.broadcast_to(jnp.sum(one, axis=1, keepdims=True), (1, 128)) for one in (tot, spread)]
    first_half = lax.broadcasted_iota(jnp.int32, (1, 128), 1) < 64
    tsum[mydev] = jnp.concatenate([moment, jnp.where(first_half, both[0], both[1])], axis=1)
    rsum[rid, 1, :, :rank] = weight
    for b in range(bands):
        rsum[rid, 0, :, b * tall : (b + 1) * tall] = jnp.sum(row_acc[b].T, axis=0, keepdims=True)

    def each(count, action):
        def body(k, carry):
            action(k)
            return carry

        lax.fori_loop(1, count, body, 0, unroll=count <= 32)

    def total_to(k):
        there = ((row + k // ncol) % nrow, (col + k % ncol) % ncol)
        send(tsum.at[mydev], tsum.at[mydev], "tsum", ("tsum",), there)

    each(nrow * ncol, total_to)
    for n in range(1, nr):
        send(rsum.at[rid], rsum.at[rid], "rsum", ("rsum",), in_plane(n))
    def to_row_group(src, dst, kind):
        for n in range(nr - 1, 0, -1):
            send(src.at[row_peer(n, 1)], dst.at[rid], kind, (kind, n), in_plane(n))

    for b in range(bands):
        psend[b * group : (b + 1) * group] = forces[b].reshape(group, rows, rank)
    to_row_group(psend, precv, "pull")
    rows_out(line_order(z, nz, nz - 1, jnp.minimum))

    def sums_to(k):
        there = ((row + k // ncol) % nrow, (col + k % ncol) % ncol)
        send(csum.at[mydev], csum.at[mydev], "csum", ("csum",), there)

    each(nrow * ncol, sums_to)

    def gram_of(block):
        return lax.dot_general(block, block, (((0,), (0,)), ((), ())), preferred_element_type=jnp.float32)

    arrive(rsum.at[pl.ds(0, nr - 1)], "rsum", ("rsum",))
    arrive(tsum.at[pl.ds(0, nrow * ncol - 1)], "tsum", ("tsum",))
    sums = jnp.sum(tsum[...], axis=0)
    moment = sums[:, :rank] / total
    grand = sums[:, rank : rank + 1] / (total * total)
    scale = 0.5 / jnp.sqrt(sums[:, rank + 64 : rank + 65] + 1e-06)
    weight = jnp.sum(rsum[:, 1], axis=0)[:, :rank]
    row_mean = jnp.sum(rsum[:, 0], axis=0) / total
    for b in range(bands):
        means[b * tall : (b + 1) * tall] = jnp.broadcast_to(row_mean[:, b * tall : (b + 1) * tall], (128, tall)).T

    own_mean = means[pl.ds(pl.multiple_of(rid * rows, rows), rows)]
    mean = jnp.concatenate([own_mean] * (rank // 128), axis=1)
    centre = 1.0 - 2.0 * mean + grand
    rounding = centre.astype(jnp.bfloat16).astype(jnp.float32) - centre
    force = mean * weight + (moment - grand * weight) - rounding * hb.astype(jnp.float32) + psend[rid]
    for n in range(1, nr):
        arrive(precv.at[row_peer(n, -1)], "pull", ("pull", n))
        force += precv[row_peer(n, -1)]
    h = jnp.maximum(h - scale * force, 0.0)

    def held(n, p):
        return later.at[(at_z(n, -1) * nr + row_peer(p, -1)) * 2 + core]

    def along_z():
        for n in range(nz - 1, 0, -1):
            send(held(0, 0), held(0, 0), "later", ("z", n), device(at_z(n, 1), y, x))

    def over_plane(n):
        block = held(n, 0)
        if n:
            arrive(block, "later", ("z", n))
        for p in range(nr - 1, 0, -1):
            if n != 1:
                send(block, block, "later", ("plane", n, p), in_plane(p))
        send(block, block, "later", ("partner", n), partner)

    def to_partner(n):
        for p in range(1, nr):
            arrive(held(n, p), "later", ("plane", n, p))
            if n == 0 and nz > 1:
                send(held(0, p), held(0, p), "later", ("plane", 1, p), device(at_z(1, 1), y, x))
            send(held(n, p), held(n, p), "later", ("partner", n), partner)

    later[(z * nr + rid) * 2 + core] = h.astype(jnp.bfloat16)
    along_z()
    over_plane(0)
    krecv[rid] = ksend[rid]
    for n in range(1, nr):
        arrive(krecv.at[row_peer(n, -1)], "kern", ("kern", n))
    arrive(csum.at[pl.ds(0, nrow * ncol - 1)], "csum", ("csum",))
    across = jnp.concatenate([own_mean] * (wide // 128), axis=1) - grand
    for q in range(nr):
        col_sum = {}
        for source in range(nz):
            for n in range(nz):
                c = line_order(source, nz, n, min)
                for one in range(2):
                    value = csum[(source * 2 + one) * ncol + q, n]
                    col_sum[c] = value + col_sum[c] if c in col_sum else value
        for c in range(nz):
            aff[q, c] = (krecv[q, c] - across - col_sum[c] / total).astype(jnp.bfloat16)
    ah = jnp.zeros((rows, rank), jnp.float32)
    hh = jnp.zeros((rank, rank), jnp.float32)

    def use(n):
        nonlocal ah, hh
        arrive(later.at[pl.ds(0, nr)], "later", ("partner", n))
        c = at_z(n, -1)
        block = later[pl.ds(c * nr * 2, nr * 2)].reshape(nr * wide, rank)
        slab = jnp.concatenate([aff[r, c] for r in range(nr)], axis=1)
        ah += jnp.dot(slab, block, preferred_element_type=jnp.float32)
        hh += gram_of(block)

    if nz > 1:
        over_plane(1)
    to_partner(0)
    for n in range(2, nz):
        over_plane(n)
    use(0)
    for n in range(1, nz):
        to_partner(n)
    for n in range(1, nz):
        use(n)
    scale = 0.5 / jnp.sqrt(jnp.sum(hh * hh, keepdims=True) + 1e-06)
    h_near, h_rest = split(h)
    hh_near, hh_rest = split(hh)
    hhh = jnp.dot(jnp.concatenate([h_near, h_rest], axis=0), hh_near, preferred_element_type=jnp.float32)
    hhh = hhh[:rows] + hhh[rows:] + jnp.dot(h_near, hh_rest, preferred_element_type=jnp.float32)
    out_ref[...] = jnp.maximum(h - scale * (hhh - ah), 0.0) / unit

    def sent(ref, kind):
        remote(ref, ref, kind, ("tsum",), partner).wait_send()

    sent(words.at[pl.ds(0, side - 1)], "word")
    sent(rbuf.at[pl.ds(0, nr - 1)], "rpts")
    sent(hr.at[pl.ds(0, nr - 1)], "rfac")
    sent(cbuf.at[pl.ds(0, nz)], "cpart")
    sent(hc.at[pl.ds(0, nz)], "hpart")
    ends = (z + nz - 1) % nz >= nz - 2
    if nz > 1:

        @pl.when(ends)
        def _():
            sent(cbuf.at[pl.ds(0, 1)], "cline")
            sent(hc.at[pl.ds(0, 1)], "hline")

    if nz > 2:

        @pl.when(jnp.logical_not(ends))
        def _():
            sent(cbuf.at[pl.ds(0, nz + 1)], "cline")
            sent(hc.at[pl.ds(0, nz + 1)], "hline")

    sent(rsum.at[pl.ds(0, nr - 1)], "rsum")
    sent(csum.at[pl.ds(0, nrow * ncol - 1)], "csum")
    sent(tsum.at[pl.ds(0, nrow * ncol - 1)], "tsum")
    sent(psend.at[pl.ds(0, nr - 1)], "pull")
    sent(ksend.at[pl.ds(0, nr - 1)], "kern")
    sent(later.at[pl.ds(0, nrow * ncol - 1)], "later")


def solution(mesh):
    nrow, ncol = mesh.shape["row"], mesh.shape["col"]
    side, nz = layout(nrow, ncol)

    def shards(points, factor):
        rows, width = points.shape
        rank = factor.shape[1]
        wide = 2 * rows
        nr = side * side
        keys = receive_keys(nrow, ncol, rows)
        buffers = [
            ((side, 8, 128), jnp.float32),
            ((nr, rows, width), jnp.bfloat16),
            ((2 * nz, rows, width), jnp.bfloat16),
            ((nr, rows, rank), jnp.bfloat16),
            ((2 * nz, rows, rank), jnp.bfloat16),
            ((nrow * ncol, rows, rank), jnp.bfloat16),
            ((nr, nz, rows, wide), jnp.float32),
            ((nr, nz, rows, wide), jnp.float32),
            ((nr, rows, rank), jnp.float32),
            ((nr, rows, rank), jnp.float32),
            ((nr, nz, rows, wide), jnp.bfloat16),
            ((nr * rows, 128), jnp.float32),
            ((nr, 2, 1, max(nr * rows, rank)), jnp.float32),
            ((nrow * ncol, nz, 1, wide), jnp.float32),
            ((nrow * ncol, 1, rank + 128), jnp.float32),
        ]
        held = sum(math.prod(shape) * jnp.dtype(kind).itemsize for shape, kind in buffers)
        return pl.pallas_call(
            functools.partial(kernel, nrow, ncol, keys),
            out_shape=jax.ShapeDtypeStruct((rows, rank), jnp.float32),
            in_specs=[pl.BlockSpec(memory_space=pltpu.VMEM)] * 2,
            out_specs=pl.BlockSpec(memory_space=pltpu.VMEM),
            scratch_shapes=[pltpu.VMEM(shape, kind) for shape, kind in buffers]
            + [pltpu.SemaphoreType.DMA((len(SENDS),)), pltpu.SemaphoreType.DMA((len(keys),))],
            compiler_params=pltpu.CompilerParams(
                collective_id=0, has_side_effects=True, vmem_limit_bytes=min(67043328, held + (16 << 20))
            ),
        )(points, factor)

    spec = P(("row", "col"), None)
    return jax.shard_map(shards, mesh=mesh, in_specs=(spec, spec), out_specs=spec, check_vma=False)
```

```python
import functools
import math

import jax
import jax.numpy as jnp
from jax import lax
from jax.experimental import pallas as pl
from jax.experimental.pallas import tpu as pltpu
from jax.sharding import PartitionSpec as P

MESH = pl.DeviceIdType.MESH

SENDS = ("word", "rpts", "cline", "cpart", "rfac", "hline", "hpart", "later", "rsum", "csum", "tsum", "pull", "kern")


def layout(nrow, ncol):
    return math.isqrt(ncol), nrow // 2


def cuts_of(rows):
    return 4 if rows % 64 == 0 else 1


def receive_keys(nrow, ncol, rows):
    side, nz = layout(nrow, ncol)
    cuts, plane = cuts_of(rows), side * side
    keys = [(name, k) for name in ("rx", "hx", "hy", "word") for k in range(1, side)]
    keys += [("ry", k, c) for k in range(1, side) for c in range(cuts)]
    keys += [("rd", j, k, c) for j in range(1, side) for k in range(1, side) for c in range(cuts)]
    keys += [("hd", j, k) for j in range(1, side) for k in range(1, side)]
    keys += [("line", k) for k in range(nz * (cuts + 1))]
    keys += [("cross", k) for k in range(nz * 2)]
    keys += [("rsum",), ("csum",), ("tsum",)]
    keys += [(name, k) for name in ("pull",) for k in range(1, plane)] + [("kern",)]
    keys += [("z", k) for k in range(1, nz)]
    keys += [("plane", k, p) for k in range(nz) for p in range(1, plane)]
    keys += [("partner", k) for k in range(nz)]
    return {key: i for i, key in enumerate(keys)}


def line_order(z, nz, n, least):
    if not n:
        return z
    up = 2 * z // nz
    sign, near = 1 - 2 * up, z + up * (nz - 1 - 2 * z)
    paired = least(near // ((n + 1) // 2), 1)
    return z + sign * (paired * (-((n + 1) // 2) if n % 2 else n // 2) + (1 - paired) * (n - near))


def shift(i, k, n, sign):
    if n & (n - 1) or n == 2:
        return (i + sign * k + n) % n
    out, bit = i, 1
    while bit < n:
        if k & bit:
            out = out + bit - 2 * bit * ((i // bit) % 2)
        bit *= 2
    return out


def kernel(nrow, ncol, keys, pts_ref, fac_ref, out_ref, words, rbuf, cbuf, hr, hc, later, ksend, krecv, psend, precv, aff, means, rsum, csum, tsum, ssem, rsem):
    side, nz = layout(nrow, ncol)
    rows, width = pts_ref.shape
    rank = fac_ref.shape[1]
    wide = 2 * rows
    nr = side * side
    total = rows * nrow * ncol
    unit = 2.0 / math.sqrt(total * rank)
    cuts = cuts_of(rows)
    piece = rows // cuts
    row, col = lax.axis_index("row"), lax.axis_index("col")
    z, core = row // 2, row % 2
    y, x = col // side, col % side
    rid = y * side + x
    partner = (z * 2 + 1 - core, col)

    def device(zz, yy, xx):
        return (zz * 2 + core, yy * side + xx)

    def at_z(k, sign):
        return shift(z, k, nz, sign)

    def at_y(k, sign):
        return (y + sign * k + side) % side

    def at_x(k, sign):
        return (x + sign * k + side) % side

    def remote(src, dst, kind, key, where):
        return pltpu.make_async_remote_copy(
            src_ref=src,
            dst_ref=dst,
            send_sem=ssem.at[SENDS.index(kind)],
            recv_sem=rsem.at[keys[key]],
            device_id=where,
            device_id_type=MESH,
        )

    def send(src, dst, kind, key, where):
        remote(src, dst, kind, key, where).start()

    def arrive(block, kind, key):
        remote(block, block, kind, key, partner).wait_recv()

    plane = [(ky, kx) for ky in range(side) for kx in range(side)]

    def row_peer(n, sign):
        ky, kx = plane[n]
        return at_y(ky, sign) * side + at_x(kx, sign)

    def in_plane(n):
        ky, kx = plane[n]
        return device(z, at_y(ky, 1), at_x(kx, 1))

    barrier = pltpu.get_barrier_semaphore()
    peers = [device(z, y, at_x(k, 1)) for k in range(1, side)]
    peers += [device(z, at_y(k, 1), x) for k in range(1, side)]
    peers.append(partner)
    for peer in peers:
        pl.semaphore_signal(barrier, inc=1, device_id=peer, device_id_type=MESH)
    not_low, not_high = z > 0, z < nz - 1

    @pl.when(not_low)
    def _():
        pl.semaphore_signal(barrier, inc=1, device_id=device(z - 1, y, x), device_id_type=MESH)

    @pl.when(not_high)
    def _():
        pl.semaphore_signal(barrier, inc=1, device_id=device(z + 1, y, x), device_id_type=MESH)

    h = fac_ref[...] * unit
    hb = h.astype(jnp.bfloat16)
    hr[rid] = hb
    hc[z * 2 + core] = hb
    rbuf[rid] = pts_ref[...]
    cbuf[z * 2 + core] = pts_ref[...]
    pl.semaphore_wait(barrier, len(peers) + jnp.minimum(z, 1) + jnp.minimum(nz - 1 - z, 1))

    def part(c):
        return pl.ds(c * piece, piece)

    def line_copy(src, c, where=None, local=None):
        block = hc.at[src * 2 + core] if c == cuts else cbuf.at[src * 2 + core, part(c)]
        return pltpu.make_async_remote_copy(
            src_ref=block if local is None else local,
            dst_ref=block,
            send_sem=ssem.at[SENDS.index("hline" if c == cuts else "cline")],
            recv_sem=rsem.at[keys["line", 0] + src * (cuts + 1) + c],
            device_id=partner if where is None else device(where, y, x),
            device_id_type=MESH,
        )

    def cross_copy(src, c, local=None):
        slot = src * 2 + core
        block = hc.at[slot] if c == cuts else cbuf.at[slot] if c is None else cbuf.at[slot, part(c)]
        return pltpu.make_async_remote_copy(
            src_ref=block if local is None else local,
            dst_ref=block,
            send_sem=ssem.at[SENDS.index("hpart" if c == cuts else "cpart")],
            recv_sem=rsem.at[keys["cross", 0] + src * 2 + (1 if c == cuts else 0)],
            device_id=partner,
            device_id_type=MESH,
        )

    def cross_wait(src):
        for block, k in ((cbuf.at[src * 2 + 1 - core], 0), (hc.at[src * 2 + 1 - core], 1)):
            pltpu.make_async_remote_copy(
                src_ref=block,
                dst_ref=block,
                send_sem=ssem.at[0],
                recv_sem=rsem.at[keys["cross", 0] + src * 2 + k],
                device_id=partner,
                device_id_type=MESH,
            ).wait_recv()

    def own_piece(c):
        local = None if c == cuts else pts_ref.at[part(c)]

        @pl.when(not_low)
        def _():
            line_copy(z, c, z - 1, local).start()

        @pl.when(not_high)
        def _():
            line_copy(z, c, z + 1, local).start()

    short = pl.ds(0, 8), pl.ds(0, 128)
    for k in range(1, side):
        send(fac_ref.at[short], words.at[y], "word", ("word", k), device(z, at_y(k, 1), x))
    order = [cuts, *range(cuts)]
    for c in order[:-1]:
        own_piece(c)
    for k in range(1, side):
        send(hr.at[rid], hr.at[rid], "rfac", ("hy", k), device(z, at_y(k, 1), x))
        send(hr.at[rid], hr.at[rid], "rfac", ("hx", k), device(z, y, at_x(k, 1)))
    for c in range(cuts):
        for k in range(1, side):
            send(pts_ref.at[part(c)], rbuf.at[rid, part(c)], "rpts", ("ry", k, c), device(z, at_y(k, 1), x))
    for k in range(1, side):
        send(pts_ref, rbuf.at[rid], "rpts", ("rx", k), device(z, y, at_x(k, 1)))
    cross_copy(z, None, pts_ref).start()
    cross_copy(z, cuts).start()

    def pass_along(d, c):
        @pl.when(z + d < nz)
        def _():
            line_copy(z + d, c).wait_recv()

            @pl.when(not_low)
            def _():
                line_copy(z + d, c, z - 1).start()

            cross_copy(z + d, c).start()

        @pl.when(z >= d)
        def _():
            line_copy(z - d, c).wait_recv()

            @pl.when(not_high)
            def _():
                line_copy(z - d, c, z + 1).start()

            cross_copy(z - d, c).start()

    def pass_over(c):
        for k in range(1, side):
            other = at_y(k, -1) * side + x
            block = hr.at[other] if c == cuts else rbuf.at[other, part(c)]
            kind, key = ("rfac", ("hy", k)) if c == cuts else ("rpts", ("ry", k, c))
            arrive(block, kind, key)
            for kx in range(1, side):
                key = ("hd", k, kx) if c == cuts else ("rd", k, kx, c)
                send(block, block, kind, key, device(z, y, at_x(kx, 1)))

    for c in order:
        if c == cuts:
            for k in range(1, side):
                arrive(words.at[at_y(k, -1)], "word", ("word", k))
            own_piece(order[-1])
        pass_over(c)
        if nz > 1:
            pass_along(1, c)
    for d in range(2, nz - 1):
        for c in order:
            pass_along(d, c)

    def squares(block):
        acc = None
        for k in range(0, width, 128):
            one = block[:, k : k + 128].astype(jnp.float32)
            acc = one * one if acc is None else acc + one * one
        return acc

    tall = min(nr * rows, 256)
    bands, group = nr * rows // tall, tall // rows
    row_sq, row_acc, forces, tots = [None] * bands, [None] * bands, [None] * bands, []
    moment = jnp.zeros((1, rank), jnp.float32)
    spread = jnp.zeros((1, 128), jnp.float32)
    weight = jnp.zeros((1, rank), jnp.float32)
    mydev = row * ncol + col

    def fold(a):
        out = a[:, :128]
        for j in range(128, a.shape[1], 128):
            out += a[:, j : j + 128]
        return out

    def split(a):
        near = a.astype(jnp.bfloat16)
        return near, (a - near.astype(jnp.float32)).astype(jnp.bfloat16)

    def plus(a, b):
        return b if a is None else a + b

    def tile(n, chip):
        nonlocal moment, spread, weight
        block = cbuf[pl.ds(chip * 2, 2)].reshape(wide, width)
        hcol = hc[pl.ds(chip * 2, 2)].reshape(wide, rank)
        col_sq = jnp.sum(squares(block).T, axis=0, keepdims=True)
        weight += jnp.sum(hcol.astype(jnp.float32), axis=0, keepdims=True)
        below = None
        for b in range(bands):
            mat = rbuf[b * group : (b + 1) * group].reshape(tall, width)
            hrow = hr[b * group : (b + 1) * group].reshape(tall, rank)
            if row_sq[b] is None:
                row_sq[b] = jnp.sum(squares(mat), axis=1, keepdims=True)
            inner = lax.dot_general(hrow, hcol, (((1,), (1,)), ((), ())), preferred_element_type=jnp.float32)
            spread += jnp.sum(fold(inner * inner), axis=0, keepdims=True)
            gram = lax.dot_general(mat, block, (((1,), (1,)), ((), ())), preferred_element_type=jnp.float32)
            k = jnp.exp((2.0 * gram - row_sq[b] - col_sq) * (0.5 / width))
            ksend[b * group : (b + 1) * group, chip] = k.reshape(group, rows, wide)
            left = jnp.concatenate([*split(k), *split(inner)], axis=0)
            prod = jnp.dot(left, hcol, preferred_element_type=jnp.float32)
            drawn = prod[:tall] + prod[tall : 2 * tall]
            moment += jnp.sum(drawn, axis=0, keepdims=True)
            forces[b] = plus(forces[b], prod[2 * tall : 3 * tall] + prod[3 * tall :] - drawn)
            row_acc[b] = plus(row_acc[b], fold(k))
            below = plus(below, jnp.sum(k, axis=0, keepdims=True))
        csum[mydev, n] = below
        tots.append(fold(below))
        if n < nz - 1:
            rows_out(chip)

    def rows_out(chip):
        for p in range(nr - 1, 0, -1):
            send(ksend.at[row_peer(p, 1), chip], krecv.at[rid, chip], "kern", ("kern",), in_plane(p))

    for k in range(1, side):
        arrive(rbuf.at[y * side + at_x(k, -1)], "rpts", ("rx", k))
        arrive(hr.at[y * side + at_x(k, -1)], "rfac", ("hx", k))
    for ky in range(1, side):
        for kx in range(1, side):
            other = at_y(ky, -1) * side + at_x(kx, -1)
            for c in range(cuts):
                arrive(rbuf.at[other, part(c)], "rpts", ("rd", ky, kx, c))
            arrive(hr.at[other], "rfac", ("hd", ky, kx))
    for n in range(nz):
        if n == nz - 1 and nz > 2:
            for c in order[1:]:
                pass_along(n, c)
        if n == nz - 2 and nz > 2:
            pass_along(nz - 1, order[0])
        chip = line_order(z, nz, n, jnp.minimum)
        cross_wait(chip)
        tile(n, chip)

    tot = sum(tots[1:], tots[0])
    both = [jnp.broadcast_to(jnp.sum(one, axis=1, keepdims=True), (1, 128)) for one in (tot, spread)]
    first_half = lax.broadcasted_iota(jnp.int32, (1, 128), 1) < 64
    tsum[mydev] = jnp.concatenate([moment, jnp.where(first_half, both[0], both[1])], axis=1)
    rsum[rid, 1, :, :rank] = weight
    for b in range(bands):
        rsum[rid, 0, :, b * tall : (b + 1) * tall] = jnp.sum(row_acc[b].T, axis=0, keepdims=True)

    def each(count, action):
        def body(k, carry):
            action(k)
            return carry

        lax.fori_loop(1, count, body, 0, unroll=count <= 32)

    def total_to(k):
        there = ((row + k // ncol) % nrow, (col + k % ncol) % ncol)
        send(tsum.at[mydev], tsum.at[mydev], "tsum", ("tsum",), there)

    each(nrow * ncol, total_to)
    for n in range(1, nr):
        send(rsum.at[rid], rsum.at[rid], "rsum", ("rsum",), in_plane(n))
    def to_row_group(src, dst, kind):
        for n in range(nr - 1, 0, -1):
            send(src.at[row_peer(n, 1)], dst.at[rid], kind, (kind, n), in_plane(n))

    for b in range(bands):
        psend[b * group : (b + 1) * group] = forces[b].reshape(group, rows, rank)
    to_row_group(psend, precv, "pull")
    rows_out(line_order(z, nz, nz - 1, jnp.minimum))

    def sums_to(k):
        there = ((row + k // ncol) % nrow, (col + k % ncol) % ncol)
        send(csum.at[mydev], csum.at[mydev], "csum", ("csum",), there)

    each(nrow * ncol, sums_to)

    def gram_of(block):
        return lax.dot_general(block, block, (((0,), (0,)), ((), ())), preferred_element_type=jnp.float32)

    arrive(rsum.at[pl.ds(0, nr - 1)], "rsum", ("rsum",))
    arrive(tsum.at[pl.ds(0, nrow * ncol - 1)], "tsum", ("tsum",))
    sums = jnp.sum(tsum[...], axis=0)
    moment = sums[:, :rank] / total
    grand = sums[:, rank : rank + 1] / (total * total)
    scale = 0.5 / jnp.sqrt(sums[:, rank + 64 : rank + 65] + 1e-06)
    weight = jnp.sum(rsum[:, 1], axis=0)[:, :rank]
    row_mean = jnp.sum(rsum[:, 0], axis=0) / total
    for b in range(bands):
        means[b * tall : (b + 1) * tall] = jnp.broadcast_to(row_mean[:, b * tall : (b + 1) * tall], (128, tall)).T

    own_mean = means[pl.ds(pl.multiple_of(rid * rows, rows), rows)]
    mean = jnp.concatenate([own_mean] * (rank // 128), axis=1)
    centre = 1.0 - 2.0 * mean + grand
    rounding = centre.astype(jnp.bfloat16).astype(jnp.float32) - centre
    force = mean * weight + (moment - grand * weight) - rounding * hb.astype(jnp.float32) + psend[rid]
    for n in range(1, nr):
        arrive(precv.at[row_peer(n, -1)], "pull", ("pull", n))
        force += precv[row_peer(n, -1)]
    h = jnp.maximum(h - scale * force, 0.0)

    def held(n, p):
        return later.at[(at_z(n, -1) * nr + row_peer(p, -1)) * 2 + core]

    def along_z():
        for n in range(nz - 1, 0, -1):
            send(held(0, 0), held(0, 0), "later", ("z", n), device(at_z(n, 1), y, x))

    def over_plane(n):
        block = held(n, 0)
        if n:
            arrive(block, "later", ("z", n))
        for p in range(nr - 1, 0, -1):
            if n != 1:
                send(block, block, "later", ("plane", n, p), in_plane(p))
        send(block, block, "later", ("partner", n), partner)

    def to_partner(n):
        for p in range(1, nr):
            arrive(held(n, p), "later", ("plane", n, p))
            if n == 0 and nz > 1:
                send(held(0, p), held(0, p), "later", ("plane", 1, p), device(at_z(1, 1), y, x))
            send(held(n, p), held(n, p), "later", ("partner", n), partner)

    later[(z * nr + rid) * 2 + core] = h.astype(jnp.bfloat16)
    along_z()
    over_plane(0)
    krecv[rid] = ksend[rid]
    arrive(krecv.at[pl.ds(0, nr - 1)], "kern", ("kern",))
    arrive(csum.at[pl.ds(0, nrow * ncol - 1)], "csum", ("csum",))
    across = jnp.concatenate([own_mean] * (wide // 128), axis=1) - grand
    for q in range(nr):
        col_sum = {}
        for source in range(nz):
            for n in range(nz):
                c = line_order(source, nz, n, min)
                for one in range(2):
                    value = csum[(source * 2 + one) * ncol + q, n]
                    col_sum[c] = value + col_sum[c] if c in col_sum else value
        for c in range(nz):
            aff[q, c] = (krecv[q, c] - across - col_sum[c] / total).astype(jnp.bfloat16)
    ah = jnp.zeros((rows, rank), jnp.float32)
    hh = jnp.zeros((rank, rank), jnp.float32)

    def use(n):
        nonlocal ah, hh
        arrive(later.at[pl.ds(0, nr)], "later", ("partner", n))
        c = at_z(n, -1)
        block = later[pl.ds(c * nr * 2, nr * 2)].reshape(nr * wide, rank)
        slab = jnp.concatenate([aff[r, c] for r in range(nr)], axis=1)
        ah += jnp.dot(slab, block, preferred_element_type=jnp.float32)
        hh += gram_of(block)

    if nz > 1:
        over_plane(1)
    to_partner(0)
    for n in range(2, nz):
        over_plane(n)
    for n in range(1, nz):
        to_partner(n)
    use(0)
    for n in range(1, nz):
        use(n)
    scale = 0.5 / jnp.sqrt(jnp.sum(hh * hh, keepdims=True) + 1e-06)
    h_near, h_rest = split(h)
    hh_near, hh_rest = split(hh)
    hhh = jnp.dot(jnp.concatenate([h_near, h_rest], axis=0), hh_near, preferred_element_type=jnp.float32)
    hhh = hhh[:rows] + hhh[rows:] + jnp.dot(h_near, hh_rest, preferred_element_type=jnp.float32)
    out_ref[...] = jnp.maximum(h - scale * (hhh - ah), 0.0) / unit

    def sent(ref, kind):
        remote(ref, ref, kind, ("tsum",), partner).wait_send()

    sent(words.at[pl.ds(0, side - 1)], "word")
    sent(rbuf.at[pl.ds(0, nr - 1)], "rpts")
    sent(hr.at[pl.ds(0, nr - 1)], "rfac")
    sent(cbuf.at[pl.ds(0, nz)], "cpart")
    sent(hc.at[pl.ds(0, nz)], "hpart")
    ends = (z + nz - 1) % nz >= nz - 2
    if nz > 1:

        @pl.when(ends)
        def _():
            sent(cbuf.at[pl.ds(0, 1)], "cline")
            sent(hc.at[pl.ds(0, 1)], "hline")

    if nz > 2:

        @pl.when(jnp.logical_not(ends))
        def _():
            sent(cbuf.at[pl.ds(0, nz + 1)], "cline")
            sent(hc.at[pl.ds(0, nz + 1)], "hline")

    sent(rsum.at[pl.ds(0, nr - 1)], "rsum")
    sent(csum.at[pl.ds(0, nrow * ncol - 1)], "csum")
    sent(tsum.at[pl.ds(0, nrow * ncol - 1)], "tsum")
    sent(psend.at[pl.ds(0, nr - 1)], "pull")
    sent(ksend.at[pl.ds(0, nr - 1)], "kern")
    sent(later.at[pl.ds(0, nrow * ncol - 1)], "later")


def solution(mesh):
    nrow, ncol = mesh.shape["row"], mesh.shape["col"]
    side, nz = layout(nrow, ncol)

    def shards(points, factor):
        rows, width = points.shape
        rank = factor.shape[1]
        wide = 2 * rows
        nr = side * side
        keys = receive_keys(nrow, ncol, rows)
        buffers = [
            ((side, 8, 128), jnp.float32),
            ((nr, rows, width), jnp.bfloat16),
            ((2 * nz, rows, width), jnp.bfloat16),
            ((nr, rows, rank), jnp.bfloat16),
            ((2 * nz, rows, rank), jnp.bfloat16),
            ((nrow * ncol, rows, rank), jnp.bfloat16),
            ((nr, nz, rows, wide), jnp.float32),
            ((nr, nz, rows, wide), jnp.float32),
            ((nr, rows, rank), jnp.float32),
            ((nr, rows, rank), jnp.float32),
            ((nr, nz, rows, wide), jnp.bfloat16),
            ((nr * rows, 128), jnp.float32),
            ((nr, 2, 1, max(nr * rows, rank)), jnp.float32),
            ((nrow * ncol, nz, 1, wide), jnp.float32),
            ((nrow * ncol, 1, rank + 128), jnp.float32),
        ]
        held = sum(math.prod(shape) * jnp.dtype(kind).itemsize for shape, kind in buffers)
        return pl.pallas_call(
            functools.partial(kernel, nrow, ncol, keys),
            out_shape=jax.ShapeDtypeStruct((rows, rank), jnp.float32),
            in_specs=[pl.BlockSpec(memory_space=pltpu.VMEM)] * 2,
            out_specs=pl.BlockSpec(memory_space=pltpu.VMEM),
            scratch_shapes=[pltpu.VMEM(shape, kind) for shape, kind in buffers]
            + [pltpu.SemaphoreType.DMA((len(SENDS),)), pltpu.SemaphoreType.DMA((len(keys),))],
            compiler_params=pltpu.CompilerParams(
                collective_id=0, has_side_effects=True, vmem_limit_bytes=min(67043328, held + (16 << 20))
            ),
        )(points, factor)

    spec = P(("row", "col"), None)
    return jax.shard_map(shards, mesh=mesh, in_specs=(spec, spec), out_specs=spec, check_vma=False)
```
